512 devices in a mesh: slab: 128 (over y, z, core), tile: 4 (over x).
Axes of the slice: x: 4, y: 4, z: 16, core: 2. Of those that a mesh axis runs over, the one named last changes fastest.
Arguments:
- tokens: bfloat16 [1024, 1024, 128], P('slab', 'tile'), may hold values from -6 to 6
- conv_weight: float32 [3, 3, 128], replicated, may hold values from -2.5 to 2.5
- occupancy: int32 [16, 16], replicated, may hold values 0 or 1
- row_gain: float32 [128], replicated, may hold values from 0.1 to 1.9
- row_qkv: bfloat16 [128, 384], replicated, may hold values from -5 to 5
- row_out: bfloat16 [128, 128], replicated, may hold values from -0.5 to 0.5
- col_gain: float32 [128], replicated, may hold values from 0.1 to 1.9
- col_qkv: bfloat16 [128, 384], replicated, may hold values from -5 to 5
- col_out: bfloat16 [128, 128], replicated, may hold values from -0.5 to 0.5
Outputs:
- mixed: bfloat16 [1024, 1024, 128], P(None, ('tile', 'slab'))
The draws below stay inside these ranges and needn't reach their ends.
All inputs are finite; a program needn't handle non-finite values.
Results may differ from the reference program's by a relative error of at most 0.02.
Values may be sent and summed in bfloat16 or wider, within the bound.
A program may use at most 64 MiB of HBM per device.

```python
import math
import jax
import jax.numpy as jnp
from jax import lax

D = 128
HEAD_DIM = 32
BLOCK = 64
COL_REACH = 128
GRID_H = 1024
GRID_W = 1024
ROW_REACH = 128


def sharp_projection(key):
    raw_draw = jnp.clip(jax.random.normal(key, (D, 3 * D), jnp.float32), -4.0, 4.0) * D ** (-0.5)
    query_part = raw_draw[:, :D]
    key_part = raw_draw[:, D:2 * D]
    value_part = raw_draw[:, 2 * D:]
    factor = jnp.full((D,), 2.0, jnp.float32)
    joined = jnp.concatenate([query_part * factor[None, :], key_part * factor[None, :], value_part], axis=1)
    return joined.astype(jnp.bfloat16)


def draw_row_qkv(key, part):
    return sharp_projection(jax.random.fold_in(key, 11))


def draw_col_qkv(key, part):
    return sharp_projection(jax.random.fold_in(key, 23))


def touch_ends(drawn, key, least, high):
    extent = drawn.shape
    index_at = [jax.random.randint(jax.random.fold_in(key, axis), (), 0, extent[axis]) for axis in range(len(extent))]
    drawn = drawn.at[tuple(index_at)].set(least)
    longest = extent.index(max(extent))
    index_at[longest] = (index_at[longest] + 1) % extent[longest]
    return drawn.at[tuple(index_at)].set(high)


def level_of(stream_key, dims, cuts, low, high):
    loudness, own = 1.0, jax.random.fold_in(stream_key, 6)
    for dim, blocks in cuts:
        heights = jnp.exp(jax.random.uniform(jax.random.fold_in(own, dim), (blocks,), jnp.float32, low / len(cuts), high / len(cuts)))
        loudness = loudness * jnp.repeat(heights, dims[dim] // blocks).reshape([-1 if axis == dim else 1 for axis in range(len(dims))])
    return loudness


def bell_draw(stream_key, dims, deviation, bound, cuts=(), kind=jnp.bfloat16):
    array = deviation * jax.random.normal(stream_key, dims, jnp.float32)
    if cuts:
        array = array * level_of(stream_key, dims, cuts, -0.22, 0.18)
    return jnp.clip(array, -bound, bound).astype(kind)


def setup_inputs(seed: int = 0) -> dict:
    seeds = jax.random.split(jax.random.key(seed), 10)
    return {
        "tokens": bell_draw(seeds[0], (GRID_H, GRID_W, D), 1.0, 6.0, ((0, 128), (1, 4))),
        "conv_weight": bell_draw(seeds[1], (3, 3, D), 0.35, 2.5, (), jnp.float32),
        "occupancy": touch_ends((jax.random.randint(seeds[2], (GRID_H // BLOCK, GRID_W // BLOCK), 0, 2) < 1).astype(jnp.int32), jax.random.fold_in(seeds[2], 1), 0, 1),
        "row_gain": jnp.clip(1.0 + 0.18 * jax.random.normal(seeds[3], (D,), jnp.float32), 0.1, 1.9),
        "row_qkv": draw_row_qkv(jax.random.fold_in(seeds[9], 71), 0),
        "row_out": bell_draw(seeds[5], (D, D), D ** -0.5, 0.5),
        "col_gain": jnp.clip(1.0 + 0.18 * jax.random.normal(seeds[6], (D,), jnp.float32), 0.1, 1.9),
        "col_qkv": draw_col_qkv(jax.random.fold_in(seeds[9], 71), 0),
        "col_out": bell_draw(seeds[8], (D, D), D ** -0.5, 0.5),
    }


def attend(queries, key_block, value_block, query_pos, key_pos, query_ok, key_ok, band_reach):
    query_count = queries.shape[0]
    key_count = key_block.shape[0]
    head_count = queries.shape[1] // HEAD_DIM
    query_heads = queries.reshape(query_count, head_count, HEAD_DIM).astype(jnp.float32)
    key_heads = key_block.reshape(key_count, head_count, HEAD_DIM).astype(jnp.float32)
    value_heads = value_block.reshape(key_count, head_count, HEAD_DIM).astype(jnp.float32)
    scores = jnp.einsum('qhd,khd->hqk', query_heads, key_heads) / math.sqrt(HEAD_DIM)
    offsets = query_pos[:, None] - key_pos[None, :]
    allowed = (jnp.abs(offsets) < band_reach) & ((key_ok[None, :] > 0) | (offsets == 0))
    scores = jnp.where(allowed[None], scores, jnp.float32(-1e+30))
    row_max = lax.optimization_barrier(jnp.max(scores, axis=-1, keepdims=True))
    exp_terms = jnp.exp(scores - row_max)
    row_total = lax.optimization_barrier(jnp.sum(exp_terms, axis=-1, keepdims=True))
    weights = (exp_terms / row_total).astype(jnp.bfloat16)
    mixture = jnp.einsum('hqk,khd->qhd', weights.astype(jnp.float32), value_heads)
    mixture = mixture * query_ok[:, None, None].astype(jnp.float32)
    return mixture.reshape(query_count, head_count * HEAD_DIM).astype(jnp.bfloat16)

def attend_line(projected, line_ok, band_reach):
    line_len = projected.shape[0]
    model_width = projected.shape[1] // 3
    block_rows = min(256, line_len)
    block_count = line_len // block_rows
    queries = projected[:, :model_width]
    key_value = jnp.pad(projected[:, model_width:], ((band_reach, band_reach), (0, 0)))
    padded_ok = jnp.pad(line_ok, (band_reach, band_reach))
    positions = jnp.arange(line_len + 2 * band_reach, dtype=jnp.int32) - band_reach

    def one_block(block_index):
        block_start = (block_index * block_rows).astype(jnp.int32)
        query_part = lax.dynamic_slice_in_dim(queries, block_start, block_rows, 0)
        query_ok = lax.dynamic_slice_in_dim(line_ok, block_start, block_rows, 0)
        query_pos = lax.dynamic_slice_in_dim(positions, block_start + band_reach, block_rows, 0)
        kv_part = lax.dynamic_slice_in_dim(key_value, block_start, block_rows + 2 * band_reach, 0)
        key_ok = lax.dynamic_slice_in_dim(padded_ok, block_start, block_rows + 2 * band_reach, 0)
        key_pos = lax.dynamic_slice_in_dim(positions, block_start, block_rows + 2 * band_reach, 0)
        return attend(query_part, kv_part[:, :model_width], kv_part[:, model_width:], query_pos, key_pos, query_ok, key_ok, band_reach)
    blocks = lax.map(one_block, jnp.arange(block_count, dtype=jnp.int32))
    return blocks.reshape(line_len, model_width)

def layer_norm(stream, gain):
    values32 = stream.astype(jnp.float32)
    center = lax.optimization_barrier(jnp.mean(values32, axis=-1, keepdims=True))
    centered = values32 - center
    spread = lax.optimization_barrier(jnp.mean(centered * centered, axis=-1, keepdims=True))
    return (centered * lax.rsqrt(spread + 1e-05) * gain).astype(jnp.bfloat16)

def sublayer(stream, occupied, gain, qkv_weight, out_weight, band_reach):
    line_count, line_len, model_width = stream.shape
    normed = layer_norm(stream, gain)
    projected = jnp.dot(normed.reshape(-1, model_width), qkv_weight, preferred_element_type=jnp.float32).astype(jnp.bfloat16)
    projected = projected.reshape(line_count, line_len, 3 * model_width)
    mixture = lax.map(lambda pieces: attend_line(pieces[0], pieces[1], band_reach), (projected, occupied))
    update = jnp.dot(mixture.reshape(-1, model_width), out_weight, preferred_element_type=jnp.float32)
    return (stream.astype(jnp.float32) + update.reshape(line_count, line_len, model_width)).astype(jnp.bfloat16)

def reference(tokens, conv_weight, occupancy, row_gain, row_qkv, row_out, col_gain, col_qkv, col_out):
    values32 = tokens.astype(jnp.float32)
    padded = jnp.pad(values32, ((1, 1), (1, 1), (0, 0)))
    convolved = values32
    for shift_row in range(3):
        for shift_col in range(3):
            convolved = convolved + conv_weight[shift_row, shift_col] * padded[shift_row:shift_row + GRID_H, shift_col:shift_col + GRID_W]
    stream = convolved.astype(jnp.bfloat16)
    occupied = jnp.repeat(jnp.repeat(occupancy, BLOCK, axis=0), BLOCK, axis=1)
    after_rows = sublayer(stream, occupied, row_gain, row_qkv, row_out, ROW_REACH)
    after_cols = sublayer(jnp.transpose(after_rows, (1, 0, 2)), occupied.T, col_gain, col_qkv, col_out, COL_REACH)
    return jnp.transpose(after_cols, (1, 0, 2))
```

```python
import math

import jax
import jax.numpy as jnp
from jax import lax
from jax.experimental import pallas as pl
from jax.experimental.pallas import tpu as pltpu
from jax.sharding import PartitionSpec as P

HEAD_DIM = 32
HEADS = 4
BLOCK = 64
REACH = 128
KEYS = 3 * REACH
NEG = -1e30
SCALE = math.log2(math.e) / math.sqrt(HEAD_DIM)


def norm(values32, gain):
    center = jnp.mean(values32, axis=-1, keepdims=True)
    centered = values32 - center
    spread = jnp.mean(centered * centered, axis=-1, keepdims=True)
    return (centered * lax.rsqrt(spread + 1e-05) * gain).astype(jnp.bfloat16)


def block_bias(key_occupied):
    lane = lax.broadcasted_iota(jnp.int32, (1, KEYS), 1) // BLOCK
    key_bias = jnp.zeros((1, KEYS), jnp.float32)
    for index, occupied in enumerate(key_occupied):
        value = jnp.where(occupied > 0, jnp.float32(0.0), jnp.float32(NEG))
        key_bias = jnp.where(lane == index, value, key_bias)
    query = lax.broadcasted_iota(jnp.int32, (REACH, KEYS), 0)
    key = lax.broadcasted_iota(jnp.int32, (REACH, KEYS), 1) - REACH
    offset = query - key
    bias = jnp.where(jnp.abs(offset) < REACH, jnp.broadcast_to(key_bias, offset.shape), NEG)
    return jnp.where(offset == 0, 0.0, bias)


def heads_of(lane_shape):
    return lax.broadcasted_iota(jnp.int32, lane_shape, 1) // HEAD_DIM


def attend_block(queries, keys, values_ones, bias, query_occupied):
    head = heads_of((REACH, 128))
    zero = jnp.zeros_like(queries)
    stacked = jnp.concatenate([jnp.where(head == h, queries, zero) for h in range(HEADS)], axis=0)
    scores = lax.dot_general(
        stacked, keys, (((1,), (1,)), ((), ())), preferred_element_type=jnp.float32
    )
    parts = []
    for h in range(HEADS):
        part = scores[h * REACH : (h + 1) * REACH] + bias
        top = jnp.max(part, axis=-1, keepdims=True)
        parts.append(jnp.exp2(part - top).astype(jnp.bfloat16))
    weights = jnp.concatenate(parts, axis=0)
    both = jnp.dot(weights, values_ones, preferred_element_type=jnp.float32)
    mixture, total = both[:REACH, :128], both[:REACH, 128:]
    for h in range(1, HEADS):
        rows = both[h * REACH : (h + 1) * REACH]
        mixture = jnp.where(head == h, rows[:, :128], mixture)
        total = jnp.where(head == h, rows[:, 128:], total)
    mixture = mixture / total
    row = lax.broadcasted_iota(jnp.int32, (REACH, 128), 0)
    occupied = jnp.where(row < BLOCK, query_occupied[0], query_occupied[1])
    return (mixture * occupied.astype(jnp.float32)).astype(jnp.bfloat16)


def occupied_at(occ_ref, row, col):
    high, wide = occ_ref.shape
    inside = (row >= 0) & (row < high) & (col >= 0) & (col < wide)
    value = occ_ref[jnp.clip(row, 0, high - 1), jnp.clip(col, 0, wide - 1)]
    return jnp.where(inside, value, 0)


def row_kernel(
    occ_ref, own_ref, top_ref, bottom_ref, left_ref, right_ref, conv_ref, gain_ref, qkv_ref, out_ref,
    after_ref, grid_s, bias_s, val_s,
):
    rows, length, width = own_ref.shape
    slab, tile = lax.axis_index("slab"), lax.axis_index("tile")
    grid_s[0, REACH : REACH + length] = top_ref[0].astype(jnp.float32)
    grid_s[1 : 1 + rows, REACH : REACH + length] = own_ref[...].astype(jnp.float32)
    grid_s[1 + rows, REACH : REACH + length] = bottom_ref[0].astype(jnp.float32)
    grid_s[:, :REACH] = left_ref[...].astype(jnp.float32)
    grid_s[:, REACH + length :] = right_ref[...].astype(jnp.float32)
    val_s[:, width:] = jnp.ones((val_s.shape[0], width), jnp.bfloat16)
    blocks = length // REACH
    occ_row = slab * rows // BLOCK
    first = tile * (length // BLOCK)
    occ = [occupied_at(occ_ref, occ_row, first - 2 + b) for b in range(2 * blocks + 4)]
    for block in range(blocks):
        bias_s[block] = block_bias(occ[2 * block : 2 * block + 6])
    taps = [[conv_ref[pl.ds(3 * a + b, 1), :] for b in range(3)] for a in range(3)]
    gain = gain_ref[...]
    count = length + 2 * REACH

    def one_row(row, carry):
        above, here, below = grid_s[row], grid_s[row + 1], grid_s[row + 2]
        left, middle, right = (
            taps[0][b] * above + taps[1][b] * here + taps[2][b] * below for b in range(3)
        )
        convolved = here + middle + pltpu.roll(left, 1, 0) + pltpu.roll(right, count - 1, 0)
        stream = convolved.astype(jnp.bfloat16).astype(jnp.float32)
        normed = norm(stream, gain)
        queries = jnp.dot(
            normed[REACH : REACH + length], qkv_ref[:, :width], preferred_element_type=jnp.float32
        )
        queries = (queries * SCALE).astype(jnp.bfloat16)
        key_value = jnp.dot(normed, qkv_ref[:, width:], preferred_element_type=jnp.float32)
        key_value = key_value.astype(jnp.bfloat16)
        keys = key_value[:, :width]
        val_s[:, :width] = key_value[:, width:]
        for block in range(blocks):
            low = block * REACH
            mixture = attend_block(
                queries[low : low + REACH],
                keys[low : low + KEYS],
                val_s[low : low + KEYS],
                bias_s[block],
                occ[2 + 2 * block : 4 + 2 * block],
            )
            update = jnp.dot(mixture, out_ref[...], preferred_element_type=jnp.float32)
            after_ref[row, low : low + REACH] = (
                stream[REACH + low : 2 * REACH + low] + update
            ).astype(jnp.bfloat16)
        return carry

    lax.fori_loop(0, rows, one_row, 0)


def col_kernel(occ_ref, x_ref, gain_ref, qkv_ref, out_ref, mixed_ref, line_s, query_s, key_s, val_s):
    count, width = x_ref.shape
    cols = key_s.shape[0]
    height = count // cols
    slab, tile = lax.axis_index("slab"), lax.axis_index("tile")
    slabs = lax.axis_size("slab")
    occ_col = (tile * slabs + slab) * cols // BLOCK
    line_s[...] = x_ref[...].astype(jnp.float32)
    gain = gain_ref[...]
    for col in range(cols):
        normed = norm(line_s[pl.ds(col, height, stride=cols), :], gain)
        queries = jnp.dot(normed, qkv_ref[:, :width], preferred_element_type=jnp.float32)
        query_s[col] = (queries * SCALE).astype(jnp.bfloat16)
        key_value = jnp.dot(normed, qkv_ref[:, width:], preferred_element_type=jnp.float32)
        key_value = key_value.astype(jnp.bfloat16)
        key_s[col, :REACH] = jnp.zeros((REACH, width), jnp.bfloat16)
        key_s[col, REACH + height :] = jnp.zeros((REACH, width), jnp.bfloat16)
        key_s[col, REACH : REACH + height] = key_value[:, :width]
        val_s[col, :REACH, :width] = jnp.zeros((REACH, width), jnp.bfloat16)
        val_s[col, REACH + height :, :width] = jnp.zeros((REACH, width), jnp.bfloat16)
        val_s[col, REACH : REACH + height, :width] = key_value[:, width:]
        val_s[col, :, width:] = jnp.ones((height + 2 * REACH, width), jnp.bfloat16)

    def one_block(block, carry):
        occ = [occupied_at(occ_ref, 2 * block - 2 + b, occ_col) for b in range(6)]
        bias = block_bias(occ)
        low = pl.multiple_of(block * REACH, REACH)
        for col in range(cols):
            mixture = attend_block(
                query_s[col, pl.ds(low, REACH)],
                key_s[col, pl.ds(low, KEYS)],
                val_s[col, pl.ds(low, KEYS)],
                bias,
                occ[2:4],
            )
            update = jnp.dot(mixture, out_ref[...], preferred_element_type=jnp.float32)
            place = pl.ds(block * (REACH * cols) + col, REACH, stride=cols)
            line_s[place, :] = line_s[place, :] + update
        return carry

    lax.fori_loop(0, height // REACH, one_block, 0)
    mixed_ref[...] = line_s[...].astype(jnp.bfloat16)


VMEM = pl.BlockSpec(memory_space=pltpu.VMEM)
SMEM = pl.BlockSpec(memory_space=pltpu.SMEM)


def exchange(block, axis, dim, width):
    count = lax.axis_size(axis)
    forward = [(i, i + 1) for i in range(count - 1)]
    backward = [(target, source) for source, target in forward]
    extent = block.shape[dim]
    low = lax.ppermute(lax.slice_in_dim(block, extent - width, extent, axis=dim), axis, forward)
    high = lax.ppermute(lax.slice_in_dim(block, 0, width, axis=dim), axis, backward)
    return low, high


def local(tokens, conv_weight, occupancy, row_gain, row_qkv, row_out, col_gain, col_qkv, col_out):
    rows, length, width = tokens.shape
    slabs = lax.axis_size("slab")
    cols = length // slabs
    height = rows * slabs
    count = length + 2 * REACH
    top, bottom = exchange(tokens, "slab", 0, 1)
    left, right = exchange(jnp.concatenate([top, tokens, bottom], axis=0), "tile", 1, REACH)
    after_rows = pl.pallas_call(
        row_kernel,
        out_shape=jax.ShapeDtypeStruct((rows, length, width), jnp.bfloat16),
        in_specs=[SMEM] + [VMEM] * 9,
        out_specs=VMEM,
        scratch_shapes=[
            pltpu.VMEM((rows + 2, count, width), jnp.float32),
            pltpu.VMEM((length // REACH, REACH, KEYS), jnp.float32),
            pltpu.VMEM((count, 2 * width), jnp.bfloat16),
        ],
        name="row_sublayer",
    )(
        occupancy, tokens, top, bottom, left, right,
        conv_weight.reshape(9, width), row_gain.reshape(1, width), row_qkv, row_out,
    )
    columns = lax.all_to_all(after_rows, "slab", split_axis=1, concat_axis=0, tiled=True)
    mixed = pl.pallas_call(
        col_kernel,
        out_shape=jax.ShapeDtypeStruct((height * cols, width), jnp.bfloat16),
        in_specs=[SMEM] + [VMEM] * 4,
        out_specs=VMEM,
        scratch_shapes=[
            pltpu.VMEM((height * cols, width), jnp.float32),
            pltpu.VMEM((cols, height, width), jnp.bfloat16),
            pltpu.VMEM((cols, height + 2 * REACH, width), jnp.bfloat16),
            pltpu.VMEM((cols, height + 2 * REACH, 2 * width), jnp.bfloat16),
        ],
        name="col_sublayer",
    )(occupancy, columns.reshape(height * cols, width), col_gain.reshape(1, width), col_qkv, col_out)
    return mixed.reshape(height, cols, width)


def solution(mesh):
    return jax.shard_map(
        local,
        mesh=mesh,
        in_specs=(P("slab", "tile", None), P(), P(), P(), P(), P(), P(), P(), P()),
        out_specs=P(None, ("tile", "slab"), None),
        check_vma=False,
    )
```

```python
import functools
import math

import jax
import jax.numpy as jnp
from jax import lax
from jax.experimental import pallas as pl
from jax.experimental.pallas import tpu as pltpu
from jax.sharding import PartitionSpec as P

HEAD_DIM = 32
HEADS = 4
BLOCK = 64
REACH = 128
KEYS = 3 * REACH
NEG = -1e30
SCALE = math.log2(math.e) / math.sqrt(HEAD_DIM)


def norm(values32, gain):
    center = jnp.mean(values32, axis=-1, keepdims=True)
    centered = values32 - center
    spread = jnp.mean(centered * centered, axis=-1, keepdims=True)
    return (centered * lax.rsqrt(spread + 1e-05) * gain).astype(jnp.bfloat16)


def block_bias(key_occupied):
    lane = lax.broadcasted_iota(jnp.int32, (1, KEYS), 1) // BLOCK
    key_bias = jnp.zeros((1, KEYS), jnp.float32)
    for index, occupied in enumerate(key_occupied):
        value = jnp.where(occupied > 0, jnp.float32(0.0), jnp.float32(NEG))
        key_bias = jnp.where(lane == index, value, key_bias)
    query = lax.broadcasted_iota(jnp.int32, (REACH, KEYS), 0)
    key = lax.broadcasted_iota(jnp.int32, (REACH, KEYS), 1) - REACH
    offset = query - key
    bias = jnp.where(jnp.abs(offset) < REACH, jnp.broadcast_to(key_bias, offset.shape), NEG)
    return jnp.where(offset == 0, 0.0, bias)


def heads_of(lane_shape):
    return lax.broadcasted_iota(jnp.int32, lane_shape, 1) // HEAD_DIM


def attend_block(queries, keys, values_ones, bias, query_occupied):
    head = heads_of((REACH, 128))
    zero = jnp.zeros_like(queries)
    stacked = jnp.concatenate([jnp.where(head == h, queries, zero) for h in range(HEADS)], axis=0)
    scores = lax.dot_general(
        stacked, keys, (((1,), (1,)), ((), ())), preferred_element_type=jnp.float32
    )
    parts = []
    for h in range(HEADS):
        part = scores[h * REACH : (h + 1) * REACH] + bias
        top = jnp.max(part, axis=-1, keepdims=True)
        parts.append(jnp.exp2(part - top).astype(jnp.bfloat16))
    weights = jnp.concatenate(parts, axis=0)
    both = jnp.dot(weights, values_ones, preferred_element_type=jnp.float32)
    mixture, total = both[:REACH, :128], both[:REACH, 128:]
    for h in range(1, HEADS):
        rows = both[h * REACH : (h + 1) * REACH]
        mixture = jnp.where(head == h, rows[:, :128], mixture)
        total = jnp.where(head == h, rows[:, 128:], total)
    mixture = mixture / total
    row = lax.broadcasted_iota(jnp.int32, (REACH, 128), 0)
    occupied = jnp.where(row < BLOCK, query_occupied[0], query_occupied[1])
    return (mixture * occupied.astype(jnp.float32)).astype(jnp.bfloat16)


def occupied_at(occ_ref, row, col):
    high, wide = occ_ref.shape
    inside = (row >= 0) & (row < high) & (col >= 0) & (col < wide)
    value = occ_ref[jnp.clip(row, 0, high - 1), jnp.clip(col, 0, wide - 1)]
    return jnp.where(inside, value, 0)


def row_kernel(
    occ_ref, own_ref, top_ref, bottom_ref, left_ref, right_ref, conv_ref, gain_ref, qkv_ref, out_ref,
    after_ref, grid_s, bias_s, val_s,
):
    rows, length, width = own_ref.shape
    slab, tile = lax.axis_index("slab"), lax.axis_index("tile")
    grid_s[0, REACH : REACH + length] = top_ref[0].astype(jnp.float32)
    grid_s[1 : 1 + rows, REACH : REACH + length] = own_ref[...].astype(jnp.float32)
    grid_s[1 + rows, REACH : REACH + length] = bottom_ref[0].astype(jnp.float32)
    grid_s[:, :REACH] = left_ref[...].astype(jnp.float32)
    grid_s[:, REACH + length :] = right_ref[...].astype(jnp.float32)
    nothing = jnp.zeros((rows + 2, REACH, width), jnp.float32)

    @pl.when(slab == 0)
    def _():
        grid_s[0] = jnp.zeros(grid_s.shape[1:], jnp.float32)

    @pl.when(slab == lax.axis_size("slab") - 1)
    def _():
        grid_s[1 + rows] = jnp.zeros(grid_s.shape[1:], jnp.float32)

    @pl.when(tile == 0)
    def _():
        grid_s[:, :REACH] = nothing

    @pl.when(tile == lax.axis_size("tile") - 1)
    def _():
        grid_s[:, REACH + length :] = nothing

    val_s[:, width:] = jnp.ones((val_s.shape[0], width), jnp.bfloat16)
    blocks = length // REACH
    occ_row = slab * rows // BLOCK
    first = tile * (length // BLOCK)
    occ = [occupied_at(occ_ref, occ_row, first - 2 + b) for b in range(2 * blocks + 4)]
    for block in range(blocks):
        bias_s[block] = block_bias(occ[2 * block : 2 * block + 6])
    taps = [[conv_ref[pl.ds(3 * a + b, 1), :] for b in range(3)] for a in range(3)]
    gain = gain_ref[...]
    count = length + 2 * REACH

    def one_row(row, carry):
        above, here, below = grid_s[row], grid_s[row + 1], grid_s[row + 2]
        left, middle, right = (
            taps[0][b] * above + taps[1][b] * here + taps[2][b] * below for b in range(3)
        )
        convolved = here + middle + pltpu.roll(left, 1, 0) + pltpu.roll(right, count - 1, 0)
        stream = convolved.astype(jnp.bfloat16).astype(jnp.float32)
        normed = norm(stream, gain)
        queries = jnp.dot(
            normed[REACH : REACH + length], qkv_ref[:, :width], preferred_element_type=jnp.float32
        )
        queries = (queries * SCALE).astype(jnp.bfloat16)
        key_value = jnp.dot(normed, qkv_ref[:, width:], preferred_element_type=jnp.float32)
        key_value = key_value.astype(jnp.bfloat16)
        keys = key_value[:, :width]
        val_s[:, :width] = key_value[:, width:]
        for block in range(blocks):
            low = block * REACH
            mixture = attend_block(
                queries[low : low + REACH],
                keys[low : low + KEYS],
                val_s[low : low + KEYS],
                bias_s[block],
                occ[2 + 2 * block : 4 + 2 * block],
            )
            update = jnp.dot(mixture, out_ref[...], preferred_element_type=jnp.float32)
            after_ref[row, low : low + REACH] = (
                stream[REACH + low : 2 * REACH + low] + update
            ).astype(jnp.bfloat16)
        return carry

    lax.fori_loop(0, rows, one_row, 0)


def col_kernel(occ_ref, x_ref, gain_ref, qkv_ref, out_ref, mixed_ref, line_s, query_s, key_s, val_s):
    count, width = x_ref.shape
    cols = key_s.shape[0]
    height = count // cols
    slab, tile = lax.axis_index("slab"), lax.axis_index("tile")
    slabs = lax.axis_size("slab")
    occ_col = (tile * slabs + slab) * cols // BLOCK
    line_s[...] = x_ref[...].astype(jnp.float32)
    gain = gain_ref[...]
    for col in range(cols):
        normed = norm(line_s[pl.ds(col, height, stride=cols), :], gain)
        queries = jnp.dot(normed, qkv_ref[:, :width], preferred_element_type=jnp.float32)
        query_s[col] = (queries * SCALE).astype(jnp.bfloat16)
        key_value = jnp.dot(normed, qkv_ref[:, width:], preferred_element_type=jnp.float32)
        key_value = key_value.astype(jnp.bfloat16)
        key_s[col, :REACH] = jnp.zeros((REACH, width), jnp.bfloat16)
        key_s[col, REACH + height :] = jnp.zeros((REACH, width), jnp.bfloat16)
        key_s[col, REACH : REACH + height] = key_value[:, :width]
        val_s[col, :REACH, :width] = jnp.zeros((REACH, width), jnp.bfloat16)
        val_s[col, REACH + height :, :width] = jnp.zeros((REACH, width), jnp.bfloat16)
        val_s[col, REACH : REACH + height, :width] = key_value[:, width:]
        val_s[col, :, width:] = jnp.ones((height + 2 * REACH, width), jnp.bfloat16)

    def one_block(block, carry):
        occ = [occupied_at(occ_ref, 2 * block - 2 + b, occ_col) for b in range(6)]
        bias = block_bias(occ)
        low = pl.multiple_of(block * REACH, REACH)
        for col in range(cols):
            mixture = attend_block(
                query_s[col, pl.ds(low, REACH)],
                key_s[col, pl.ds(low, KEYS)],
                val_s[col, pl.ds(low, KEYS)],
                bias,
                occ[2:4],
            )
            update = jnp.dot(mixture, out_ref[...], preferred_element_type=jnp.float32)
            place = pl.ds(block * (REACH * cols) + col, REACH, stride=cols)
            line_s[place, :] = line_s[place, :] + update
        return carry

    lax.fori_loop(0, height // REACH, one_block, 0)
    mixed_ref[...] = line_s[...].astype(jnp.bfloat16)


VMEM = pl.BlockSpec(memory_space=pltpu.VMEM)
SMEM = pl.BlockSpec(memory_space=pltpu.SMEM)


ANY = pl.BlockSpec(memory_space=pl.ANY)
MESH = pl.DeviceIdType.MESH


def halo_kernel(own_ref, top_ref, bottom_ref, left_ref, right_ref, send_sem, recv_sem):
    rows, length, width = own_ref.shape
    slabs, tiles = lax.axis_size("slab"), lax.axis_size("tile")
    slab, tile = lax.axis_index("slab"), lax.axis_index("tile")
    down, up = lax.rem(slab + 1, slabs), lax.rem(slab + slabs - 1, slabs)
    east, west = lax.rem(tile + 1, tiles), lax.rem(tile + tiles - 1, tiles)
    low, high = pl.ds(0, REACH), pl.ds(length - REACH, REACH)
    first, last, inner = pl.ds(0, 1), pl.ds(rows - 1, 1), pl.ds(1, rows)
    after = pl.ds(rows + 1, 1)
    plan = [
        (own_ref.at[:, high], left_ref.at[inner], (slab, east)),
        (own_ref.at[:, low], right_ref.at[inner], (slab, west)),
        (own_ref.at[last, high], left_ref.at[first], (down, east)),
        (own_ref.at[last, low], right_ref.at[first], (down, west)),
        (own_ref.at[first, high], left_ref.at[after], (up, east)),
        (own_ref.at[first, low], right_ref.at[after], (up, west)),
        (own_ref.at[last], top_ref, (down, tile)),
        (own_ref.at[first], bottom_ref, (up, tile)),
    ]
    barrier = pltpu.get_barrier_semaphore()
    for _, _, device in plan:
        pl.semaphore_signal(barrier, inc=1, device_id=device, device_id_type=MESH)
    pl.semaphore_wait(barrier, len(plan))
    copies = [
        pltpu.make_async_remote_copy(
            src_ref=source, dst_ref=target, send_sem=send_sem.at[k], recv_sem=recv_sem.at[k],
            device_id=device, device_id_type=MESH,
        )
        for k, (source, target, device) in enumerate(plan)
    ]
    for copy in copies:
        copy.start()
    for copy in copies:
        copy.wait()


def swap_kernel(slabs, after_ref, columns_ref, own_sem, send_sem, recv_sem):
    rows = after_ref.shape[0]
    slab, tile = lax.axis_index("slab"), lax.axis_index("tile")
    barrier = pltpu.get_barrier_semaphore()

    def greet(k, carry):
        device = (lax.rem(slab + k, slabs), tile)
        pl.semaphore_signal(barrier, inc=1, device_id=device, device_id_type=MESH)
        return carry

    lax.fori_loop(1, slabs, greet, 0)
    place = pl.ds(slab * rows, rows)
    own = pltpu.make_async_copy(after_ref.at[:, slab], columns_ref.at[place], own_sem)
    own.start()
    pl.semaphore_wait(barrier, slabs - 1)

    def send(k, carry):
        step = (k + 1) // 2
        to = lax.rem(slab + lax.rem(k, 2) * step + (1 - lax.rem(k, 2)) * (slabs - step), slabs)
        pltpu.make_async_remote_copy(
            src_ref=after_ref.at[:, to], dst_ref=columns_ref.at[place],
            send_sem=send_sem, recv_sem=recv_sem, device_id=(to, tile), device_id_type=MESH,
        ).start()
        return carry

    lax.fori_loop(1, slabs, send, 0)
    own.wait()
    sent = columns_ref.at[pl.ds(0, (slabs - 1) * rows)]
    whole = pltpu.make_async_remote_copy(
        src_ref=sent, dst_ref=sent, send_sem=send_sem, recv_sem=recv_sem,
        device_id=(lax.rem(slab + 1, slabs), tile), device_id_type=MESH,
    )
    whole.wait_send()
    whole.wait_recv()


def local(tokens, conv_weight, occupancy, row_gain, row_qkv, row_out, col_gain, col_qkv, col_out):
    rows, length, width = tokens.shape
    slabs = lax.axis_size("slab")
    cols = length // slabs
    height = rows * slabs
    count = length + 2 * REACH
    edge = jax.ShapeDtypeStruct((1, length, width), tokens.dtype)
    side = jax.ShapeDtypeStruct((rows + 2, REACH, width), tokens.dtype)
    top, bottom, left, right = pl.pallas_call(
        halo_kernel,
        out_shape=(edge, edge, side, side),
        in_specs=[ANY],
        out_specs=(ANY,) * 4,
        scratch_shapes=[pltpu.SemaphoreType.DMA((8,)), pltpu.SemaphoreType.DMA((8,))],
        compiler_params=pltpu.CompilerParams(collective_id=0, has_side_effects=True),
        name="halo",
    )(tokens)
    after_rows = pl.pallas_call(
        row_kernel,
        out_shape=jax.ShapeDtypeStruct((rows, length, width), jnp.bfloat16),
        in_specs=[SMEM] + [VMEM] * 9,
        out_specs=VMEM,
        scratch_shapes=[
            pltpu.VMEM((rows + 2, count, width), jnp.float32),
            pltpu.VMEM((length // REACH, REACH, KEYS), jnp.float32),
            pltpu.VMEM((count, 2 * width), jnp.bfloat16),
        ],
        name="row_sublayer",
    )(
        occupancy, tokens, top, bottom, left, right,
        conv_weight.reshape(9, width), row_gain.reshape(1, width), row_qkv, row_out,
    )
    columns = pl.pallas_call(
        functools.partial(swap_kernel, slabs),
        out_shape=jax.ShapeDtypeStruct((height, cols, width), jnp.bfloat16),
        in_specs=[VMEM],
        out_specs=ANY,
        scratch_shapes=[pltpu.SemaphoreType.DMA] * 3,
        compiler_params=pltpu.CompilerParams(collective_id=1, has_side_effects=True),
        name="swap",
    )(after_rows.reshape(rows, slabs, cols, width))
    mixed = pl.pallas_call(
        col_kernel,
        out_shape=jax.ShapeDtypeStruct((height * cols, width), jnp.bfloat16),
        in_specs=[SMEM] + [VMEM] * 4,
        out_specs=VMEM,
        scratch_shapes=[
            pltpu.VMEM((height * cols, width), jnp.float32),
            pltpu.VMEM((cols, height, width), jnp.bfloat16),
            pltpu.VMEM((cols, height + 2 * REACH, width), jnp.bfloat16),
            pltpu.VMEM((cols, height + 2 * REACH, 2 * width), jnp.bfloat16),
        ],
        name="col_sublayer",
    )(occupancy, columns.reshape(height * cols, width), col_gain.reshape(1, width), col_qkv, col_out)
    return mixed.reshape(height, cols, width)


def solution(mesh):
    return jax.shard_map(
        local,
        mesh=mesh,
        in_specs=(P("slab", "tile", None), P(), P(), P(), P(), P(), P(), P(), P()),
        out_specs=P(None, ("tile", "slab"), None),
        check_vma=False,
    )
```

```python
import math

import jax
import jax.numpy as jnp
from jax import lax
from jax.experimental import pallas as pl
from jax.experimental.pallas import tpu as pltpu
from jax.sharding import PartitionSpec as P

HEAD_DIM = 32
HEADS = 4
BLOCK = 64
REACH = 128
KEYS = 3 * REACH
GROUP = 4
NEG = -1e30
SCALE = math.log2(math.e) / math.sqrt(HEAD_DIM)


def norm(values32, gain):
    center = jnp.mean(values32, axis=-1, keepdims=True)
    centered = values32 - center
    spread = jnp.mean(centered * centered, axis=-1, keepdims=True)
    return (centered * lax.rsqrt(spread + 1e-05) * gain).astype(jnp.bfloat16)


def block_bias(key_occupied):
    lane = lax.broadcasted_iota(jnp.int32, (1, KEYS), 1) // BLOCK
    key_bias = jnp.zeros((1, KEYS), jnp.float32)
    for index, occupied in enumerate(key_occupied):
        value = jnp.where(occupied > 0, jnp.float32(0.0), jnp.float32(NEG))
        key_bias = jnp.where(lane == index, value, key_bias)
    query = lax.broadcasted_iota(jnp.int32, (REACH, KEYS), 0)
    key = lax.broadcasted_iota(jnp.int32, (REACH, KEYS), 1) - REACH
    offset = query - key
    bias = jnp.where(jnp.abs(offset) < REACH, jnp.broadcast_to(key_bias, offset.shape), NEG)
    return jnp.where(offset == 0, 0.0, bias)


def heads_of(lane_shape):
    return lax.broadcasted_iota(jnp.int32, lane_shape, 1) // HEAD_DIM


def attend_block(queries, keys, values_ones, bias, query_occupied):
    head = heads_of((REACH, 128))
    zero = jnp.zeros_like(queries)
    stacked = jnp.concatenate([jnp.where(head == h, queries, zero) for h in range(HEADS)], axis=0)
    scores = lax.dot_general(
        stacked, keys, (((1,), (1,)), ((), ())), preferred_element_type=jnp.float32
    )
    parts = []
    for h in range(HEADS):
        part = scores[h * REACH : (h + 1) * REACH] + bias
        top = jnp.max(part, axis=-1, keepdims=True)
        parts.append(jnp.exp2(part - top).astype(jnp.bfloat16))
    weights = jnp.concatenate(parts, axis=0)
    both = jnp.dot(weights, values_ones, preferred_element_type=jnp.float32)
    mixture, total = both[:REACH, :128], both[:REACH, 128:]
    for h in range(1, HEADS):
        rows = both[h * REACH : (h + 1) * REACH]
        mixture = jnp.where(head == h, rows[:, :128], mixture)
        total = jnp.where(head == h, rows[:, 128:], total)
    mixture = mixture / total
    row = lax.broadcasted_iota(jnp.int32, (REACH, 128), 0)
    occupied = jnp.where(row < BLOCK, query_occupied[0], query_occupied[1])
    return (mixture * occupied.astype(jnp.float32)).astype(jnp.bfloat16)


def occupied_at(occ_ref, row, col):
    high, wide = occ_ref.shape
    inside = (row >= 0) & (row < high) & (col >= 0) & (col < wide)
    value = occ_ref[jnp.clip(row, 0, high - 1), jnp.clip(col, 0, wide - 1)]
    return jnp.where(inside, value, 0)


def row_kernel(
    occ_ref, own_ref, top_ref, bottom_ref, left_ref, right_ref, conv_ref, gain_ref, qkv_ref, out_ref,
    columns_ref, grid_s, bias_s, val_s, after_s, own_sem, send_sem, recv_sem,
):
    rows, length, width = own_ref.shape
    slabs, cols = after_s.shape[1:3]
    slab, tile = lax.axis_index("slab"), lax.axis_index("tile")
    barrier = pltpu.get_barrier_semaphore()

    def greet(k, carry):
        device = (lax.rem(slab + k, slabs), tile)
        pl.semaphore_signal(barrier, inc=1, device_id=device, device_id_type=MESH)
        return carry

    lax.fori_loop(1, slabs, greet, 0)
    grid_s[0, REACH : REACH + length] = top_ref[0].astype(jnp.float32)
    grid_s[1 : 1 + rows, REACH : REACH + length] = own_ref[...].astype(jnp.float32)
    grid_s[1 + rows, REACH : REACH + length] = bottom_ref[0].astype(jnp.float32)
    grid_s[:, :REACH] = left_ref[...].astype(jnp.float32)
    grid_s[:, REACH + length :] = right_ref[...].astype(jnp.float32)
    nothing = jnp.zeros((rows + 2, REACH, width), jnp.float32)

    @pl.when(slab == 0)
    def _():
        grid_s[0] = jnp.zeros(grid_s.shape[1:], jnp.float32)

    @pl.when(slab == lax.axis_size("slab") - 1)
    def _():
        grid_s[1 + rows] = jnp.zeros(grid_s.shape[1:], jnp.float32)

    @pl.when(tile == 0)
    def _():
        grid_s[:, :REACH] = nothing

    @pl.when(tile == lax.axis_size("tile") - 1)
    def _():
        grid_s[:, REACH + length :] = nothing

    val_s[:, width:] = jnp.ones((val_s.shape[0], width), jnp.bfloat16)
    blocks = length // REACH
    occ_row = slab * rows // BLOCK
    first = tile * (length // BLOCK)
    occ = [occupied_at(occ_ref, occ_row, first - 2 + b) for b in range(2 * blocks + 4)]
    for block in range(blocks):
        bias_s[block] = block_bias(occ[2 * block : 2 * block + 6])
    taps = [[conv_ref[pl.ds(3 * a + b, 1), :] for b in range(3)] for a in range(3)]
    gain = gain_ref[...]
    count = length + 2 * REACH

    def one_row(row, carry):
        above, here, below = grid_s[row], grid_s[row + 1], grid_s[row + 2]
        left, middle, right = (
            taps[0][b] * above + taps[1][b] * here + taps[2][b] * below for b in range(3)
        )
        convolved = here + middle + pltpu.roll(left, 1, 0) + pltpu.roll(right, count - 1, 0)
        stream = convolved.astype(jnp.bfloat16).astype(jnp.float32)
        normed = norm(stream, gain)
        queries = jnp.dot(
            normed[REACH : REACH + length], qkv_ref[:, :width], preferred_element_type=jnp.float32
        )
        queries = (queries * SCALE).astype(jnp.bfloat16)
        key_value = jnp.dot(normed, qkv_ref[:, width:], preferred_element_type=jnp.float32)
        key_value = key_value.astype(jnp.bfloat16)
        keys = key_value[:, :width]
        val_s[:, :width] = key_value[:, width:]
        for block in range(blocks):
            low = block * REACH
            mixture = attend_block(
                queries[low : low + REACH],
                keys[low : low + KEYS],
                val_s[low : low + KEYS],
                bias_s[block],
                occ[2 + 2 * block : 4 + 2 * block],
            )
            update = jnp.dot(mixture, out_ref[...], preferred_element_type=jnp.float32)
            result = stream[REACH + low : 2 * REACH + low] + update
            after_s[row, low // cols : (low + REACH) // cols] = result.reshape(
                REACH // cols, cols, width
            ).astype(jnp.bfloat16)
        return carry

    for group in range(rows // GROUP):
        start = group * GROUP
        lax.fori_loop(start, start + GROUP, one_row, 0)
        if group == 0:
            pl.semaphore_wait(barrier, slabs - 1)
        taken = pl.ds(start, GROUP)
        place = pl.ds(slab * rows + start, GROUP)
        pltpu.make_async_copy(
            after_s.at[taken, slab], columns_ref.at[place], own_sem.at[group]
        ).start()

        def send(k, carry):
            step = (k + 1) // 2
            to = lax.rem(slab + lax.rem(k, 2) * step + (1 - lax.rem(k, 2)) * (slabs - step), slabs)
            pltpu.make_async_remote_copy(
                src_ref=after_s.at[taken, to], dst_ref=columns_ref.at[place],
                send_sem=send_sem, recv_sem=recv_sem, device_id=(to, tile), device_id_type=MESH,
            ).start()
            return carry

        lax.fori_loop(1, slabs, send, 0)
    for group in range(rows // GROUP):
        start = group * GROUP
        pltpu.make_async_copy(
            after_s.at[pl.ds(start, GROUP), slab],
            columns_ref.at[pl.ds(slab * rows + start, GROUP)],
            own_sem.at[group],
        ).wait()
    sent = columns_ref.at[pl.ds(0, (slabs - 1) * rows)]
    whole = pltpu.make_async_remote_copy(
        src_ref=sent, dst_ref=sent, send_sem=send_sem, recv_sem=recv_sem,
        device_id=(lax.rem(slab + 1, slabs), tile), device_id_type=MESH,
    )
    whole.wait_send()
    whole.wait_recv()


def col_kernel(occ_ref, x_ref, gain_ref, qkv_ref, out_ref, mixed_ref, line_s, query_s, key_s, val_s):
    count, width = x_ref.shape
    cols = key_s.shape[0]
    height = count // cols
    slab, tile = lax.axis_index("slab"), lax.axis_index("tile")
    slabs = lax.axis_size("slab")
    occ_col = (tile * slabs + slab) * cols // BLOCK
    line_s[...] = x_ref[...].astype(jnp.float32)
    gain = gain_ref[...]
    for col in range(cols):
        normed = norm(line_s[pl.ds(col, height, stride=cols), :], gain)
        queries = jnp.dot(normed, qkv_ref[:, :width], preferred_element_type=jnp.float32)
        query_s[col] = (queries * SCALE).astype(jnp.bfloat16)
        key_value = jnp.dot(normed, qkv_ref[:, width:], preferred_element_type=jnp.float32)
        key_value = key_value.astype(jnp.bfloat16)
        key_s[col, :REACH] = jnp.zeros((REACH, width), jnp.bfloat16)
        key_s[col, REACH + height :] = jnp.zeros((REACH, width), jnp.bfloat16)
        key_s[col, REACH : REACH + height] = key_value[:, :width]
        val_s[col, :REACH, :width] = jnp.zeros((REACH, width), jnp.bfloat16)
        val_s[col, REACH + height :, :width] = jnp.zeros((REACH, width), jnp.bfloat16)
        val_s[col, REACH : REACH + height, :width] = key_value[:, width:]
        val_s[col, :, width:] = jnp.ones((height + 2 * REACH, width), jnp.bfloat16)

    def one_block(block, carry):
        occ = [occupied_at(occ_ref, 2 * block - 2 + b, occ_col) for b in range(6)]
        bias = block_bias(occ)
        low = pl.multiple_of(block * REACH, REACH)
        for col in range(cols):
            mixture = attend_block(
                query_s[col, pl.ds(low, REACH)],
                key_s[col, pl.ds(low, KEYS)],
                val_s[col, pl.ds(low, KEYS)],
                bias,
                occ[2:4],
            )
            update = jnp.dot(mixture, out_ref[...], preferred_element_type=jnp.float32)
            place = pl.ds(block * (REACH * cols) + col, REACH, stride=cols)
            line_s[place, :] = line_s[place, :] + update
        return carry

    lax.fori_loop(0, height // REACH, one_block, 0)
    mixed_ref[...] = line_s[...].astype(jnp.bfloat16)


VMEM = pl.BlockSpec(memory_space=pltpu.VMEM)
SMEM = pl.BlockSpec(memory_space=pltpu.SMEM)


ANY = pl.BlockSpec(memory_space=pl.ANY)
MESH = pl.DeviceIdType.MESH


def halo_kernel(own_ref, top_ref, bottom_ref, left_ref, right_ref, send_sem, recv_sem):
    rows, length, width = own_ref.shape
    slabs, tiles = lax.axis_size("slab"), lax.axis_size("tile")
    slab, tile = lax.axis_index("slab"), lax.axis_index("tile")
    down, up = lax.rem(slab + 1, slabs), lax.rem(slab + slabs - 1, slabs)
    east, west = lax.rem(tile + 1, tiles), lax.rem(tile + tiles - 1, tiles)
    low, high = pl.ds(0, REACH), pl.ds(length - REACH, REACH)
    first, last, inner = pl.ds(0, 1), pl.ds(rows - 1, 1), pl.ds(1, rows)
    after = pl.ds(rows + 1, 1)
    plan = [
        (own_ref.at[:, high], left_ref.at[inner], (slab, east)),
        (own_ref.at[:, low], right_ref.at[inner], (slab, west)),
        (own_ref.at[last, high], left_ref.at[first], (down, east)),
        (own_ref.at[last, low], right_ref.at[first], (down, west)),
        (own_ref.at[first, high], left_ref.at[after], (up, east)),
        (own_ref.at[first, low], right_ref.at[after], (up, west)),
        (own_ref.at[last], top_ref, (down, tile)),
        (own_ref.at[first], bottom_ref, (up, tile)),
    ]
    barrier = pltpu.get_barrier_semaphore()
    for _, _, device in plan:
        pl.semaphore_signal(barrier, inc=1, device_id=device, device_id_type=MESH)
    pl.semaphore_wait(barrier, len(plan))
    copies = [
        pltpu.make_async_remote_copy(
            src_ref=source, dst_ref=target, send_sem=send_sem.at[k], recv_sem=recv_sem.at[k],
            device_id=device, device_id_type=MESH,
        )
        for k, (source, target, device) in enumerate(plan)
    ]
    for copy in copies:
        copy.start()
    for copy in copies:
        copy.wait()


def local(tokens, conv_weight, occupancy, row_gain, row_qkv, row_out, col_gain, col_qkv, col_out):
    rows, length, width = tokens.shape
    slabs = lax.axis_size("slab")
    cols = length // slabs
    height = rows * slabs
    count = length + 2 * REACH
    edge = jax.ShapeDtypeStruct((1, length, width), tokens.dtype)
    side = jax.ShapeDtypeStruct((rows + 2, REACH, width), tokens.dtype)
    top, bottom, left, right = pl.pallas_call(
        halo_kernel,
        out_shape=(edge, edge, side, side),
        in_specs=[ANY],
        out_specs=(ANY,) * 4,
        scratch_shapes=[pltpu.SemaphoreType.DMA((8,)), pltpu.SemaphoreType.DMA((8,))],
        compiler_params=pltpu.CompilerParams(collective_id=0, has_side_effects=True),
        name="halo",
    )(tokens)
    columns = pl.pallas_call(
        row_kernel,
        out_shape=jax.ShapeDtypeStruct((height, cols, width), jnp.bfloat16),
        in_specs=[SMEM] + [VMEM] * 9,
        out_specs=ANY,
        scratch_shapes=[
            pltpu.VMEM((rows + 2, count, width), jnp.float32),
            pltpu.VMEM((length // REACH, REACH, KEYS), jnp.float32),
            pltpu.VMEM((count, 2 * width), jnp.bfloat16),
            pltpu.VMEM((rows, slabs, cols, width), jnp.bfloat16),
            pltpu.SemaphoreType.DMA((rows // GROUP,)),
            pltpu.SemaphoreType.DMA,
            pltpu.SemaphoreType.DMA,
        ],
        compiler_params=pltpu.CompilerParams(collective_id=1, has_side_effects=True),
        name="row_sublayer",
    )(
        occupancy, tokens, top, bottom, left, right,
        conv_weight.reshape(9, width), row_gain.reshape(1, width), row_qkv, row_out,
    )
    mixed = pl.pallas_call(
        col_kernel,
        out_shape=jax.ShapeDtypeStruct((height * cols, width), jnp.bfloat16),
        in_specs=[SMEM] + [VMEM] * 4,
        out_specs=VMEM,
        scratch_shapes=[
            pltpu.VMEM((height * cols, width), jnp.float32),
            pltpu.VMEM((cols, height, width), jnp.bfloat16),
            pltpu.VMEM((cols, height + 2 * REACH, width), jnp.bfloat16),
            pltpu.VMEM((cols, height + 2 * REACH, 2 * width), jnp.bfloat16),
        ],
        name="col_sublayer",
    )(occupancy, columns.reshape(height * cols, width), col_gain.reshape(1, width), col_qkv, col_out)
    return mixed.reshape(height, cols, width)


def solution(mesh):
    return jax.shard_map(
        local,
        mesh=mesh,
        in_specs=(P("slab", "tile", None), P(), P(), P(), P(), P(), P(), P(), P()),
        out_specs=P(None, ("tile", "slab"), None),
        check_vma=False,
    )
```

```python
import math

import jax
import jax.numpy as jnp
from jax import lax
from jax.experimental import pallas as pl
from jax.experimental.pallas import tpu as pltpu
from jax.sharding import PartitionSpec as P

HEAD_DIM = 32
HEADS = 4
BLOCK = 64
REACH = 128
KEYS = 3 * REACH
GROUP = 4
NEG = -1e30
SCALE = math.log2(math.e) / math.sqrt(HEAD_DIM)


def norm(values32, gain):
    center = jnp.mean(values32, axis=-1, keepdims=True)
    centered = values32 - center
    spread = jnp.mean(centered * centered, axis=-1, keepdims=True)
    return (centered * lax.rsqrt(spread + 1e-05) * gain).astype(jnp.bfloat16)


def block_bias(key_occupied):
    at = lax.broadcasted_iota(jnp.int32, (KEYS, REACH), 0)
    key_bias = jnp.zeros((KEYS, REACH), jnp.float32)
    for index, occupied in enumerate(key_occupied):
        value = jnp.where(occupied > 0, jnp.float32(0.0), jnp.float32(NEG))
        key_bias = jnp.where(at // BLOCK == index, value, key_bias)
    offset = lax.broadcasted_iota(jnp.int32, (KEYS, REACH), 1) - (at - REACH)
    bias = jnp.where(jnp.abs(offset) < REACH, key_bias, NEG)
    return jnp.where(offset == 0, 0.0, bias)


def attend_block(queries, keys, values_t, bias, query_occupied, out_weight):
    head = lax.broadcasted_iota(jnp.int32, (REACH, 128), 1) // HEAD_DIM
    zero = jnp.zeros_like(queries)
    stacked = jnp.concatenate([jnp.where(head == h, queries, zero) for h in range(HEADS)], axis=0)
    scores = lax.dot_general(
        keys, stacked, (((1,), (1,)), ((), ())), preferred_element_type=jnp.float32
    )
    lane = lax.broadcasted_iota(jnp.int32, (1, REACH), 1)
    occupied = jnp.where(lane < BLOCK, query_occupied[0], query_occupied[1]).astype(jnp.float32)
    mixtures = []
    for h in range(HEADS):
        part = scores[:, h * REACH : (h + 1) * REACH] + bias
        weights = jnp.exp2(part - jnp.max(part, axis=0, keepdims=True))
        total = jnp.sum(weights, axis=0, keepdims=True)
        mixture = jnp.dot(
            values_t[h * HEAD_DIM : (h + 1) * HEAD_DIM],
            weights.astype(jnp.bfloat16),
            preferred_element_type=jnp.float32,
        )
        mixtures.append(mixture * (occupied / total))
    mixture = jnp.concatenate(mixtures, axis=0).T.astype(jnp.bfloat16)
    return jnp.dot(mixture, out_weight, preferred_element_type=jnp.float32)


def project(normed, qkv_ref, width):
    both = jnp.dot(normed, qkv_ref[:, : 2 * width], preferred_element_type=jnp.float32)
    values_t = lax.dot_general(
        qkv_ref[:, 2 * width :], normed, (((0,), (1,)), ((), ())), preferred_element_type=jnp.float32
    )
    queries = (both[:, :width] * SCALE).astype(jnp.bfloat16)
    return queries, both[:, width:].astype(jnp.bfloat16), values_t.astype(jnp.bfloat16)


def occupied_at(occ_ref, row, col):
    high, wide = occ_ref.shape
    inside = (row >= 0) & (row < high) & (col >= 0) & (col < wide)
    value = occ_ref[jnp.clip(row, 0, high - 1), jnp.clip(col, 0, wide - 1)]
    return jnp.where(inside, value, 0)


def row_kernel(
    occ_ref, own_ref, top_ref, bottom_ref, left_ref, right_ref, conv_ref, gain_ref, qkv_ref, out_ref,
    columns_ref, grid_s, bias_s, after_s, own_sem, send_sem, recv_sem,
):
    rows, length, width = own_ref.shape
    slabs, cols = after_s.shape[1:3]
    slab, tile = lax.axis_index("slab"), lax.axis_index("tile")
    barrier = pltpu.get_barrier_semaphore()

    def greet(k, carry):
        to = slab + k
        device = (jnp.where(to >= slabs, to - slabs, to), tile)
        pl.semaphore_signal(barrier, inc=1, device_id=device, device_id_type=MESH)
        return carry

    lax.fori_loop(1, slabs, greet, 0)
    grid_s[0, REACH : REACH + length] = top_ref[0].astype(jnp.float32)
    grid_s[1 : 1 + rows, REACH : REACH + length] = own_ref[...].astype(jnp.float32)
    grid_s[1 + rows, REACH : REACH + length] = bottom_ref[0].astype(jnp.float32)
    grid_s[:, :REACH] = left_ref[...].astype(jnp.float32)
    grid_s[:, REACH + length :] = right_ref[...].astype(jnp.float32)
    nothing = jnp.zeros((rows + 2, REACH, width), jnp.float32)

    @pl.when(slab == 0)
    def _():
        grid_s[0] = jnp.zeros(grid_s.shape[1:], jnp.float32)

    @pl.when(slab == lax.axis_size("slab") - 1)
    def _():
        grid_s[1 + rows] = jnp.zeros(grid_s.shape[1:], jnp.float32)

    @pl.when(tile == 0)
    def _():
        grid_s[:, :REACH] = nothing

    @pl.when(tile == lax.axis_size("tile") - 1)
    def _():
        grid_s[:, REACH + length :] = nothing

    blocks = length // REACH
    occ_row = slab * rows // BLOCK
    first = tile * (length // BLOCK)
    occ = [occupied_at(occ_ref, occ_row, first - 2 + b) for b in range(2 * blocks + 4)]
    for block in range(blocks):
        bias_s[block] = block_bias(occ[2 * block : 2 * block + 6])
    taps = [[conv_ref[a, pl.ds(b, 1), :] for b in range(3)] for a in range(3)]
    gain = gain_ref[...]
    count = length + 2 * REACH

    def one_row(row, carry):
        above, here, below = grid_s[row], grid_s[row + 1], grid_s[row + 2]
        left, middle, right = (
            taps[0][b] * above + taps[1][b] * here + taps[2][b] * below for b in range(3)
        )
        convolved = here + middle + pltpu.roll(left, 1, 0) + pltpu.roll(right, count - 1, 0)
        stream = convolved.astype(jnp.bfloat16).astype(jnp.float32)
        normed = norm(stream, gain)
        queries, keys, values_t = project(normed, qkv_ref, width)
        for block in range(blocks):
            low = block * REACH
            update = attend_block(
                queries[REACH + low : 2 * REACH + low],
                keys[low : low + KEYS],
                values_t[:, low : low + KEYS],
                bias_s[block],
                occ[2 + 2 * block : 4 + 2 * block],
                out_ref[...],
            )
            result = stream[REACH + low : 2 * REACH + low] + update
            after_s[row, low // cols : (low + REACH) // cols] = result.reshape(
                REACH // cols, cols, width
            ).astype(jnp.bfloat16)
        return carry

    for group in range(rows // GROUP):
        start = group * GROUP
        lax.fori_loop(start, start + GROUP, one_row, 0)
        if group == 0:
            pl.semaphore_wait(barrier, slabs - 1)
        taken = pl.ds(start, GROUP)
        place = pl.ds(slab * rows + start, GROUP)
        pltpu.make_async_copy(
            after_s.at[taken, slab], columns_ref.at[place], own_sem.at[group]
        ).start()

        def send(to):
            pltpu.make_async_remote_copy(
                src_ref=after_s.at[taken, to], dst_ref=columns_ref.at[place],
                send_sem=send_sem, recv_sem=recv_sem, device_id=(to, tile), device_id_type=MESH,
            ).start()

        def send_both(step, carry):
            ahead, behind = slab + step, slab - step
            send(jnp.where(ahead >= slabs, ahead - slabs, ahead))
            send(jnp.where(behind < 0, behind + slabs, behind))
            return carry

        lax.fori_loop(1, slabs // 2, send_both, 0, unroll=3)
        half = slab + slabs // 2
        send(jnp.where(half >= slabs, half - slabs, half))
    for group in range(rows // GROUP):
        start = group * GROUP
        pltpu.make_async_copy(
            after_s.at[pl.ds(start, GROUP), slab],
            columns_ref.at[pl.ds(slab * rows + start, GROUP)],
            own_sem.at[group],
        ).wait()
    sent = columns_ref.at[pl.ds(0, (slabs - 1) * rows)]
    whole = pltpu.make_async_remote_copy(
        src_ref=sent, dst_ref=sent, send_sem=send_sem, recv_sem=recv_sem,
        device_id=(lax.rem(slab + 1, slabs), tile), device_id_type=MESH,
    )
    whole.wait_send()
    whole.wait_recv()


def col_kernel(occ_ref, x_ref, gain_ref, qkv_ref, out_ref, mixed_ref, line_s, query_s, key_s, val_s):
    count, width = x_ref.shape
    cols = key_s.shape[0]
    height = count // cols
    slab, tile = lax.axis_index("slab"), lax.axis_index("tile")
    slabs = lax.axis_size("slab")
    occ_col = (tile * slabs + slab) * cols // BLOCK
    line_s[...] = x_ref[...].astype(jnp.float32)
    gain = gain_ref[...]
    for col in range(cols):
        normed = norm(line_s[pl.ds(col, height, stride=cols), :], gain)
        query_s[col], keys, values_t = project(normed, qkv_ref, width)
        edge = jnp.zeros((REACH, width), jnp.bfloat16)
        key_s[col, :REACH], key_s[col, REACH + height :] = edge, edge
        val_s[col, :, :REACH], val_s[col, :, REACH + height :] = edge, edge
        key_s[col, REACH : REACH + height] = keys
        val_s[col, :, REACH : REACH + height] = values_t

    def one_block(block, carry):
        occ = [occupied_at(occ_ref, 2 * block - 2 + b, occ_col) for b in range(6)]
        bias = block_bias(occ)
        low = pl.multiple_of(block * REACH, REACH)
        for col in range(cols):
            update = attend_block(
                query_s[col, pl.ds(low, REACH)],
                key_s[col, pl.ds(low, KEYS)],
                val_s[col, :, pl.ds(low, KEYS)],
                bias,
                occ[2:4],
                out_ref[...],
            )
            place = pl.ds(block * (REACH * cols) + col, REACH, stride=cols)
            line_s[place, :] = line_s[place, :] + update
        return carry

    lax.fori_loop(0, height // REACH, one_block, 0)
    mixed_ref[...] = line_s[...].astype(jnp.bfloat16)


VMEM = pl.BlockSpec(memory_space=pltpu.VMEM)
SMEM = pl.BlockSpec(memory_space=pltpu.SMEM)


ANY = pl.BlockSpec(memory_space=pl.ANY)
MESH = pl.DeviceIdType.MESH


def halo_kernel(own_ref, top_ref, bottom_ref, left_ref, right_ref, send_sem, recv_sem):
    rows, length, width = own_ref.shape
    slabs, tiles = lax.axis_size("slab"), lax.axis_size("tile")
    slab, tile = lax.axis_index("slab"), lax.axis_index("tile")
    down, up = lax.rem(slab + 1, slabs), lax.rem(slab + slabs - 1, slabs)
    east, west = lax.rem(tile + 1, tiles), lax.rem(tile + tiles - 1, tiles)
    low, high = pl.ds(0, REACH), pl.ds(length - REACH, REACH)
    first, last, inner = pl.ds(0, 1), pl.ds(rows - 1, 1), pl.ds(1, rows)
    after = pl.ds(rows + 1, 1)
    plan = [
        (own_ref.at[:, high], left_ref.at[inner], (slab, east)),
        (own_ref.at[:, low], right_ref.at[inner], (slab, west)),
        (own_ref.at[last, high], left_ref.at[first], (down, east)),
        (own_ref.at[last, low], right_ref.at[first], (down, west)),
        (own_ref.at[first, high], left_ref.at[after], (up, east)),
        (own_ref.at[first, low], right_ref.at[after], (up, west)),
        (own_ref.at[last], top_ref, (down, tile)),
        (own_ref.at[first], bottom_ref, (up, tile)),
    ]
    barrier = pltpu.get_barrier_semaphore()
    for _, _, device in plan:
        pl.semaphore_signal(barrier, inc=1, device_id=device, device_id_type=MESH)
    pl.semaphore_wait(barrier, len(plan))
    copies = [
        pltpu.make_async_remote_copy(
            src_ref=source, dst_ref=target, send_sem=send_sem.at[k], recv_sem=recv_sem.at[k],
            device_id=device, device_id_type=MESH,
        )
        for k, (source, target, device) in enumerate(plan)
    ]
    for copy in copies:
        copy.start()
    for copy in copies:
        copy.wait()


def local(tokens, conv_weight, occupancy, row_gain, row_qkv, row_out, col_gain, col_qkv, col_out):
    rows, length, width = tokens.shape
    slabs = lax.axis_size("slab")
    cols = length // slabs
    height = rows * slabs
    count = length + 2 * REACH
    edge = jax.ShapeDtypeStruct((1, length, width), tokens.dtype)
    side = jax.ShapeDtypeStruct((rows + 2, REACH, width), tokens.dtype)
    top, bottom, left, right = pl.pallas_call(
        halo_kernel,
        out_shape=(edge, edge, side, side),
        in_specs=[ANY],
        out_specs=(ANY,) * 4,
        scratch_shapes=[pltpu.SemaphoreType.DMA((8,)), pltpu.SemaphoreType.DMA((8,))],
        compiler_params=pltpu.CompilerParams(collective_id=0, has_side_effects=True),
        name="halo",
    )(tokens)
    columns = pl.pallas_call(
        row_kernel,
        out_shape=jax.ShapeDtypeStruct((height, cols, width), jnp.bfloat16),
        in_specs=[SMEM] + [VMEM] * 9,
        out_specs=ANY,
        scratch_shapes=[
            pltpu.VMEM((rows + 2, count, width), jnp.float32),
            pltpu.VMEM((length // REACH, KEYS, REACH), jnp.float32),
            pltpu.VMEM((rows, slabs, cols, width), jnp.bfloat16),
            pltpu.SemaphoreType.DMA((rows // GROUP,)),
            pltpu.SemaphoreType.DMA,
            pltpu.SemaphoreType.DMA,
        ],
        compiler_params=pltpu.CompilerParams(collective_id=1, has_side_effects=True),
        name="row_sublayer",
    )(
        occupancy, tokens, top, bottom, left, right,
        conv_weight, row_gain.reshape(1, width), row_qkv, row_out,
    )
    mixed = pl.pallas_call(
        col_kernel,
        out_shape=jax.ShapeDtypeStruct((height * cols, width), jnp.bfloat16),
        in_specs=[SMEM] + [VMEM] * 4,
        out_specs=VMEM,
        scratch_shapes=[
            pltpu.VMEM((height * cols, width), jnp.float32),
            pltpu.VMEM((cols, height, width), jnp.bfloat16),
            pltpu.VMEM((cols, height + 2 * REACH, width), jnp.bfloat16),
            pltpu.VMEM((cols, width, height + 2 * REACH), jnp.bfloat16),
        ],
        name="col_sublayer",
    )(occupancy, columns.reshape(height * cols, width), col_gain.reshape(1, width), col_qkv, col_out)
    return mixed.reshape(height, cols, width)


def solution(mesh):
    return jax.shard_map(
        local,
        mesh=mesh,
        in_specs=(P("slab", "tile", None), P(), P(), P(), P(), P(), P(), P(), P()),
        out_specs=P(None, ("tile", "slab"), None),
        check_vma=False,
    )
```

```python
import math

import jax
import jax.numpy as jnp
from jax import lax
from jax.experimental import pallas as pl
from jax.experimental.pallas import tpu as pltpu
from jax.sharding import PartitionSpec as P

HEAD_DIM = 32
HEADS = 4
BLOCK = 64
REACH = 128
KEYS = 3 * REACH
GROUP = 4
NEG = -1e30
SCALE = math.log2(math.e) / math.sqrt(HEAD_DIM)


def norm(values32, gain):
    center = jnp.mean(values32, axis=-1, keepdims=True)
    centered = values32 - center
    spread = jnp.mean(centered * centered, axis=-1, keepdims=True)
    return (centered * lax.rsqrt(spread + 1e-05) * gain).astype(jnp.bfloat16)


def block_bias(key_occupied):
    at = lax.broadcasted_iota(jnp.int32, (KEYS, REACH), 0)
    key_bias = jnp.zeros((KEYS, REACH), jnp.float32)
    for index, occupied in enumerate(key_occupied):
        value = jnp.where(occupied > 0, jnp.float32(0.0), jnp.float32(NEG))
        key_bias = jnp.where(at // BLOCK == index, value, key_bias)
    offset = lax.broadcasted_iota(jnp.int32, (KEYS, REACH), 1) - (at - REACH)
    bias = jnp.where(jnp.abs(offset) < REACH, key_bias, NEG)
    return jnp.where(offset == 0, 0.0, bias)


def attend_block(queries, keys, values_t, bias, query_occupied, out_weight):
    head = lax.broadcasted_iota(jnp.int32, (REACH, 128), 1) // HEAD_DIM
    zero = jnp.zeros_like(queries)
    stacked = jnp.concatenate([jnp.where(head == h, queries, zero) for h in range(HEADS)], axis=0)
    scores = lax.dot_general(
        keys, stacked, (((1,), (1,)), ((), ())), preferred_element_type=jnp.float32
    )
    lane = lax.broadcasted_iota(jnp.int32, (1, REACH), 1)
    occupied = jnp.where(lane < BLOCK, query_occupied[0], query_occupied[1]).astype(jnp.float32)
    mixtures = []
    for h in range(HEADS):
        part = scores[:, h * REACH : (h + 1) * REACH] + bias
        weights = jnp.exp2(part - jnp.max(part, axis=0, keepdims=True))
        total = jnp.sum(weights, axis=0, keepdims=True)
        mixture = jnp.dot(
            values_t[h * HEAD_DIM : (h + 1) * HEAD_DIM],
            weights.astype(jnp.bfloat16),
            preferred_element_type=jnp.float32,
        )
        mixtures.append(mixture * (occupied / total))
    mixture = jnp.concatenate(mixtures, axis=0).T.astype(jnp.bfloat16)
    return jnp.dot(mixture, out_weight, preferred_element_type=jnp.float32)


SPAN = BLOCK + 2 * REACH


def attend_small(queries, keys, values_t, bias, out_weight):
    head = lax.broadcasted_iota(jnp.int32, (BLOCK, 128), 1) // HEAD_DIM
    zero = jnp.zeros_like(queries)
    stacked = jnp.concatenate([jnp.where(head == h, queries, zero) for h in range(HEADS)], axis=0)
    scores = lax.dot_general(
        keys, stacked, (((1,), (1,)), ((), ())), preferred_element_type=jnp.float32
    )
    mixtures = []
    for pair in range(HEADS // 2):
        part = scores[:, pair * 128 : (pair + 1) * 128] + bias
        weights = jnp.exp2(part - jnp.max(part, axis=0, keepdims=True))
        total = jnp.sum(weights, axis=0, keepdims=True)
        mixture = jnp.dot(
            values_t[pair * BLOCK : (pair + 1) * BLOCK],
            weights.astype(jnp.bfloat16),
            preferred_element_type=jnp.float32,
        )
        mixtures.append(mixture * (1.0 / total))
    both = jnp.concatenate(mixtures, axis=0).T
    mixture = jnp.where(head % 2 == 0, both[:BLOCK], both[BLOCK:]).astype(jnp.bfloat16)
    return jnp.dot(mixture, out_weight, preferred_element_type=jnp.float32)


def project(normed, qkv_ref, width):
    both = jnp.dot(normed, qkv_ref[:, : 2 * width], preferred_element_type=jnp.float32)
    values_t = lax.dot_general(
        qkv_ref[:, 2 * width :], normed, (((0,), (1,)), ((), ())), preferred_element_type=jnp.float32
    )
    queries = (both[:, :width] * SCALE).astype(jnp.bfloat16)
    return queries, both[:, width:].astype(jnp.bfloat16), values_t.astype(jnp.bfloat16)


def occupied_at(occ_ref, row, col):
    high, wide = occ_ref.shape
    inside = (row >= 0) & (row < high) & (col >= 0) & (col < wide)
    value = occ_ref[jnp.clip(row, 0, high - 1), jnp.clip(col, 0, wide - 1)]
    return jnp.where(inside, value, 0)


def row_kernel(
    occ_ref, own_ref, top_ref, bottom_ref, left_ref, right_ref, conv_ref, gain_ref, qkv_ref, out_ref,
    columns_ref, grid_s, bias_s, after_s, own_sem, send_sem, recv_sem,
):
    rows, length, width = own_ref.shape
    slabs, cols = after_s.shape[1:3]
    slab, tile = lax.axis_index("slab"), lax.axis_index("tile")
    barrier = pltpu.get_barrier_semaphore()

    def greet(k, carry):
        to = slab + k
        device = (jnp.where(to >= slabs, to - slabs, to), tile)
        pl.semaphore_signal(barrier, inc=1, device_id=device, device_id_type=MESH)
        return carry

    lax.fori_loop(1, slabs, greet, 0)
    grid_s[0, REACH : REACH + length] = top_ref[0].astype(jnp.float32)
    grid_s[1 : 1 + rows, REACH : REACH + length] = own_ref[...].astype(jnp.float32)
    grid_s[1 + rows, REACH : REACH + length] = bottom_ref[0].astype(jnp.float32)
    grid_s[:, :REACH] = left_ref[...].astype(jnp.float32)
    grid_s[:, REACH + length :] = right_ref[...].astype(jnp.float32)
    nothing = jnp.zeros((rows + 2, REACH, width), jnp.float32)

    @pl.when(slab == 0)
    def _():
        grid_s[0] = jnp.zeros(grid_s.shape[1:], jnp.float32)

    @pl.when(slab == lax.axis_size("slab") - 1)
    def _():
        grid_s[1 + rows] = jnp.zeros(grid_s.shape[1:], jnp.float32)

    @pl.when(tile == 0)
    def _():
        grid_s[:, :REACH] = nothing

    @pl.when(tile == lax.axis_size("tile") - 1)
    def _():
        grid_s[:, REACH + length :] = nothing

    blocks = length // REACH
    occ_row = slab * rows // BLOCK
    first = tile * (length // BLOCK)
    occ = [occupied_at(occ_ref, occ_row, first - 2 + b) for b in range(2 * blocks + 4)]
    for block in range(blocks):
        bias_s[block] = block_bias(occ[2 * block : 2 * block + 6])
    taps = [[conv_ref[a, pl.ds(b, 1), :] for b in range(3)] for a in range(3)]
    gain = gain_ref[...]
    count = length + 2 * REACH

    def one_row(row, carry):
        above, here, below = grid_s[row], grid_s[row + 1], grid_s[row + 2]
        left, middle, right = (
            taps[0][b] * above + taps[1][b] * here + taps[2][b] * below for b in range(3)
        )
        convolved = here + middle + pltpu.roll(left, 1, 0) + pltpu.roll(right, count - 1, 0)
        stream = convolved.astype(jnp.bfloat16).astype(jnp.float32)
        normed = norm(stream, gain)
        queries, keys, values_t = project(normed, qkv_ref, width)
        for block in range(blocks):
            low = block * REACH
            update = attend_block(
                queries[REACH + low : 2 * REACH + low],
                keys[low : low + KEYS],
                values_t[:, low : low + KEYS],
                bias_s[block],
                occ[2 + 2 * block : 4 + 2 * block],
                out_ref[...],
            )
            result = stream[REACH + low : 2 * REACH + low] + update
            after_s[row, low // cols : (low + REACH) // cols] = result.reshape(
                REACH // cols, cols, width
            ).astype(jnp.bfloat16)
        return carry

    for group in range(rows // GROUP):
        start = group * GROUP
        lax.fori_loop(start, start + GROUP, one_row, 0)
        if group == 0:
            pl.semaphore_wait(barrier, slabs - 1)
        taken = pl.ds(start, GROUP)
        place = pl.ds(slab * rows + start, GROUP)
        pltpu.make_async_copy(
            after_s.at[taken, slab], columns_ref.at[place], own_sem.at[group]
        ).start()

        def send(to):
            pltpu.make_async_remote_copy(
                src_ref=after_s.at[taken, to], dst_ref=columns_ref.at[place],
                send_sem=send_sem, recv_sem=recv_sem, device_id=(to, tile), device_id_type=MESH,
            ).start()

        def send_both(step, carry):
            ahead, behind = slab + step, slab - step
            send(jnp.where(ahead >= slabs, ahead - slabs, ahead))
            send(jnp.where(behind < 0, behind + slabs, behind))
            return carry

        lax.fori_loop(1, slabs // 2, send_both, 0, unroll=3)
        half = slab + slabs // 2
        send(jnp.where(half >= slabs, half - slabs, half))
    for group in range(rows // GROUP):
        start = group * GROUP
        pltpu.make_async_copy(
            after_s.at[pl.ds(start, GROUP), slab],
            columns_ref.at[pl.ds(slab * rows + start, GROUP)],
            own_sem.at[group],
        ).wait()
    sent = columns_ref.at[pl.ds(0, (slabs - 1) * rows)]
    whole = pltpu.make_async_remote_copy(
        src_ref=sent, dst_ref=sent, send_sem=send_sem, recv_sem=recv_sem,
        device_id=(lax.rem(slab + 1, slabs), tile), device_id_type=MESH,
    )
    whole.wait_send()
    whole.wait_recv()


def col_kernel(occ_ref, x_ref, gain_ref, qkv_ref, out_ref, mixed_ref, line_s, query_s, key_s, val_s, blocks_s):
    count, width = x_ref.shape
    cols = key_s.shape[0]
    height = count // cols
    slab, tile = lax.axis_index("slab"), lax.axis_index("tile")
    slabs = lax.axis_size("slab")
    occ_col = (tile * slabs + slab) * cols // BLOCK
    line_s[...] = x_ref[...].astype(jnp.float32)
    gain = gain_ref[...]
    for col in range(cols):
        normed = norm(line_s[pl.ds(col, height, stride=cols), :], gain)
        query_s[col], keys, values_t = project(normed, qkv_ref, width)
        edge = jnp.zeros((REACH, width), jnp.bfloat16)
        key_s[col, :REACH], key_s[col, REACH + height :] = edge, edge
        key_s[col, REACH : REACH + height] = keys
        wide = jnp.concatenate([edge, values_t, edge], axis=1)
        val_s[0, col] = wide
        val_s[1, col, :, : height + REACH] = wide[:, BLOCK : BLOCK + height + REACH]
        val_s[1, col, :, height + REACH :] = edge

    at = lax.broadcasted_iota(jnp.int32, (SPAN, 128), 0)
    offset = lax.broadcasted_iota(jnp.int32, (SPAN, 128), 1) % BLOCK - (at - REACH)
    band = jnp.where(jnp.abs(offset) < REACH, jnp.float32(0.0), jnp.float32(NEG))

    total_blocks = height // BLOCK

    def note(block, found):
        blocks_s[found] = block
        return found + jnp.where(occupied_at(occ_ref, block, occ_col) > 0, 1, 0)

    found = lax.fori_loop(0, total_blocks, note, 0)

    @pl.when(found < total_blocks)
    def _():
        blocks_s[found] = 0

    def updates_of(block):
        occ = [occupied_at(occ_ref, block - 2 + b, occ_col) for b in range(5)]
        barred = [
            jnp.full((BLOCK, 128), jnp.where(value > 0, jnp.float32(0.0), jnp.float32(NEG)))
            for value in occ
        ]
        bias = jnp.where(offset == 0, 0.0, jnp.minimum(band, jnp.concatenate(barred, axis=0)))
        low = pl.multiple_of(block * BLOCK, BLOCK)
        wide_low = pl.multiple_of(block // 2 * REACH, REACH)
        return [
            attend_small(
                query_s[col, pl.ds(low, BLOCK)],
                key_s[col, pl.ds(low, SPAN)],
                val_s[block % 2, col, :, pl.ds(wide_low, KEYS)][:, :SPAN],
                bias,
                out_ref[...],
            )
            for col in range(cols)
        ]

    def add(block, updates):
        for col in range(cols):
            place = pl.ds(block * (BLOCK * cols) + col, BLOCK, stride=cols)
            line_s[place, :] = line_s[place, :] + updates[col]

    def two_blocks(pair, carry):
        one, two = blocks_s[2 * pair], blocks_s[2 * pair + 1]
        first, second = updates_of(one), updates_of(two)
        add(one, first)

        @pl.when(2 * pair + 1 < found)
        def _():
            add(two, second)

        return carry

    lax.fori_loop(0, (found + 1) // 2, two_blocks, 0)
    mixed_ref[...] = line_s[...].astype(jnp.bfloat16)


VMEM = pl.BlockSpec(memory_space=pltpu.VMEM)
SMEM = pl.BlockSpec(memory_space=pltpu.SMEM)


ANY = pl.BlockSpec(memory_space=pl.ANY)
MESH = pl.DeviceIdType.MESH


def halo_kernel(own_ref, top_ref, bottom_ref, left_ref, right_ref, send_sem, recv_sem):
    rows, length, width = own_ref.shape
    slabs, tiles = lax.axis_size("slab"), lax.axis_size("tile")
    slab, tile = lax.axis_index("slab"), lax.axis_index("tile")
    down, up = lax.rem(slab + 1, slabs), lax.rem(slab + slabs - 1, slabs)
    east, west = lax.rem(tile + 1, tiles), lax.rem(tile + tiles - 1, tiles)
    low, high = pl.ds(0, REACH), pl.ds(length - REACH, REACH)
    first, last, inner = pl.ds(0, 1), pl.ds(rows - 1, 1), pl.ds(1, rows)
    after = pl.ds(rows + 1, 1)
    plan = [
        (own_ref.at[:, high], left_ref.at[inner], (slab, east)),
        (own_ref.at[:, low], right_ref.at[inner], (slab, west)),
        (own_ref.at[last, high], left_ref.at[first], (down, east)),
        (own_ref.at[last, low], right_ref.at[first], (down, west)),
        (own_ref.at[first, high], left_ref.at[after], (up, east)),
        (own_ref.at[first, low], right_ref.at[after], (up, west)),
        (own_ref.at[last], top_ref, (down, tile)),
        (own_ref.at[first], bottom_ref, (up, tile)),
    ]
    barrier = pltpu.get_barrier_semaphore()
    for _, _, device in plan:
        pl.semaphore_signal(barrier, inc=1, device_id=device, device_id_type=MESH)
    pl.semaphore_wait(barrier, len(plan))
    copies = [
        pltpu.make_async_remote_copy(
            src_ref=source, dst_ref=target, send_sem=send_sem.at[k], recv_sem=recv_sem.at[k],
            device_id=device, device_id_type=MESH,
        )
        for k, (source, target, device) in enumerate(plan)
    ]
    for copy in copies:
        copy.start()
    for copy in copies:
        copy.wait()


def local(tokens, conv_weight, occupancy, row_gain, row_qkv, row_out, col_gain, col_qkv, col_out):
    rows, length, width = tokens.shape
    slabs = lax.axis_size("slab")
    cols = length // slabs
    height = rows * slabs
    count = length + 2 * REACH
    edge = jax.ShapeDtypeStruct((1, length, width), tokens.dtype)
    side = jax.ShapeDtypeStruct((rows + 2, REACH, width), tokens.dtype)
    top, bottom, left, right = pl.pallas_call(
        halo_kernel,
        out_shape=(edge, edge, side, side),
        in_specs=[ANY],
        out_specs=(ANY,) * 4,
        scratch_shapes=[pltpu.SemaphoreType.DMA((8,)), pltpu.SemaphoreType.DMA((8,))],
        compiler_params=pltpu.CompilerParams(collective_id=0, has_side_effects=True),
        name="halo",
    )(tokens)
    columns = pl.pallas_call(
        row_kernel,
        out_shape=jax.ShapeDtypeStruct((height, cols, width), jnp.bfloat16),
        in_specs=[SMEM] + [VMEM] * 9,
        out_specs=ANY,
        scratch_shapes=[
            pltpu.VMEM((rows + 2, count, width), jnp.float32),
            pltpu.VMEM((length // REACH, KEYS, REACH), jnp.float32),
            pltpu.VMEM((rows, slabs, cols, width), jnp.bfloat16),
            pltpu.SemaphoreType.DMA((rows // GROUP,)),
            pltpu.SemaphoreType.DMA,
            pltpu.SemaphoreType.DMA,
        ],
        compiler_params=pltpu.CompilerParams(collective_id=1, has_side_effects=True),
        name="row_sublayer",
    )(
        occupancy, tokens, top, bottom, left, right,
        conv_weight, row_gain.reshape(1, width), row_qkv, row_out,
    )
    mixed = pl.pallas_call(
        col_kernel,
        out_shape=jax.ShapeDtypeStruct((height * cols, width), jnp.bfloat16),
        in_specs=[SMEM] + [VMEM] * 4,
        out_specs=VMEM,
        scratch_shapes=[
            pltpu.VMEM((height * cols, width), jnp.float32),
            pltpu.VMEM((cols, height, width), jnp.bfloat16),
            pltpu.VMEM((cols, height + 2 * REACH, width), jnp.bfloat16),
            pltpu.VMEM((2, cols, width, height + 2 * REACH), jnp.bfloat16),
            pltpu.SMEM((height // BLOCK,), jnp.int32),
        ],
        name="col_sublayer",
    )(occupancy, columns.reshape(height * cols, width), col_gain.reshape(1, width), col_qkv, col_out)
    return mixed.reshape(height, cols, width)


def solution(mesh):
    return jax.shard_map(
        local,
        mesh=mesh,
        in_specs=(P("slab", "tile", None), P(), P(), P(), P(), P(), P(), P(), P()),
        out_specs=P(None, ("tile", "slab"), None),
        check_vma=False,
    )
```

```python
import math

import jax
import jax.numpy as jnp
from jax import lax
from jax.experimental import pallas as pl
from jax.experimental.pallas import tpu as pltpu
from jax.sharding import PartitionSpec as P

HEAD_DIM = 32
HEADS = 4
BLOCK = 64
REACH = 128
KEYS = 3 * REACH
GROUP = 2
NEG = -1e30
SCALE = math.log2(math.e) / math.sqrt(HEAD_DIM)


def norm(values32, gain):
    center = jnp.mean(values32, axis=-1, keepdims=True)
    centered = values32 - center
    spread = jnp.mean(centered * centered, axis=-1, keepdims=True)
    return (centered * lax.rsqrt(spread + 1e-05) * gain).astype(jnp.bfloat16)


def block_bias(key_occupied):
    at = lax.broadcasted_iota(jnp.int32, (KEYS, REACH), 0)
    key_bias = jnp.zeros((KEYS, REACH), jnp.float32)
    for index, occupied in enumerate(key_occupied):
        value = jnp.where(occupied > 0, jnp.float32(0.0), jnp.float32(NEG))
        key_bias = jnp.where(at // BLOCK == index, value, key_bias)
    offset = lax.broadcasted_iota(jnp.int32, (KEYS, REACH), 1) - (at - REACH)
    bias = jnp.where(jnp.abs(offset) < REACH, key_bias, NEG)
    return jnp.where(offset == 0, 0.0, bias)


def attend_block(queries, keys, values_t, bias, query_occupied, out_weight):
    head = lax.broadcasted_iota(jnp.int32, (REACH, 128), 1) // HEAD_DIM
    zero = jnp.zeros_like(queries)
    stacked = jnp.concatenate([jnp.where(head == h, queries, zero) for h in range(HEADS)], axis=0)
    scores = lax.dot_general(
        keys, stacked, (((1,), (1,)), ((), ())), preferred_element_type=jnp.float32
    )
    lane = lax.broadcasted_iota(jnp.int32, (1, REACH), 1)
    occupied = jnp.where(lane < BLOCK, query_occupied[0], query_occupied[1]).astype(jnp.float32)
    mixtures = []
    for h in range(HEADS):
        part = scores[:, h * REACH : (h + 1) * REACH] + bias
        weights = jnp.exp2(part - jnp.max(part, axis=0, keepdims=True))
        total = jnp.sum(weights, axis=0, keepdims=True)
        mixture = jnp.dot(
            values_t[h * HEAD_DIM : (h + 1) * HEAD_DIM],
            weights.astype(jnp.bfloat16),
            preferred_element_type=jnp.float32,
        )
        mixtures.append(mixture * (occupied / total))
    mixture = jnp.concatenate(mixtures, axis=0).T.astype(jnp.bfloat16)
    return jnp.dot(mixture, out_weight, preferred_element_type=jnp.float32)


SPAN = BLOCK + 2 * REACH


def attend_small(queries, keys, values_t, bias, out_weight):
    head = lax.broadcasted_iota(jnp.int32, (BLOCK, 128), 1) // HEAD_DIM
    zero = jnp.zeros_like(queries)
    stacked = jnp.concatenate([jnp.where(head == h, queries, zero) for h in range(HEADS)], axis=0)
    scores = lax.dot_general(
        keys, stacked, (((1,), (1,)), ((), ())), preferred_element_type=jnp.float32
    )
    mixtures = []
    for pair in range(HEADS // 2):
        part = scores[:, pair * 128 : (pair + 1) * 128] + bias
        weights = jnp.exp2(part - jnp.max(part, axis=0, keepdims=True))
        total = jnp.sum(weights, axis=0, keepdims=True)
        mixture = jnp.dot(
            values_t[pair * BLOCK : (pair + 1) * BLOCK],
            weights.astype(jnp.bfloat16),
            preferred_element_type=jnp.float32,
        )
        mixtures.append(mixture * (1.0 / total))
    both = jnp.concatenate(mixtures, axis=0).T
    mixture = jnp.where(head % 2 == 0, both[:BLOCK], both[BLOCK:]).astype(jnp.bfloat16)
    return jnp.dot(mixture, out_weight, preferred_element_type=jnp.float32)


def project(normed, qkv_ref, width):
    both = jnp.dot(normed, qkv_ref[:, : 2 * width], preferred_element_type=jnp.float32)
    values_t = lax.dot_general(
        qkv_ref[:, 2 * width :], normed, (((0,), (1,)), ((), ())), preferred_element_type=jnp.float32
    )
    queries = (both[:, :width] * SCALE).astype(jnp.bfloat16)
    return queries, both[:, width:].astype(jnp.bfloat16), values_t.astype(jnp.bfloat16)


def occupied_at(occ_ref, row, col):
    high, wide = occ_ref.shape
    inside = (row >= 0) & (row < high) & (col >= 0) & (col < wide)
    value = occ_ref[jnp.clip(row, 0, high - 1), jnp.clip(col, 0, wide - 1)]
    return jnp.where(inside, value, 0)


def row_kernel(
    occ_ref, own_ref, top_ref, bottom_ref, left_ref, right_ref, conv_ref, gain_ref, qkv_ref, out_ref,
    columns_ref, grid_s, bias_s, after_s, own_sem, send_sem, recv_sem,
):
    rows, length, width = own_ref.shape
    slabs, cols = after_s.shape[1:3]
    slab, tile = lax.axis_index("slab"), lax.axis_index("tile")
    barrier = pltpu.get_barrier_semaphore()

    def greet(k, carry):
        to = slab + k
        device = (jnp.where(to >= slabs, to - slabs, to), tile)
        pl.semaphore_signal(barrier, inc=1, device_id=device, device_id_type=MESH)
        return carry

    lax.fori_loop(1, slabs, greet, 0)
    grid_s[0, REACH : REACH + length] = top_ref[0].astype(jnp.float32)
    grid_s[1 : 1 + rows, REACH : REACH + length] = own_ref[...].astype(jnp.float32)
    grid_s[1 + rows, REACH : REACH + length] = bottom_ref[0].astype(jnp.float32)
    grid_s[:, :REACH] = left_ref[...].astype(jnp.float32)
    grid_s[:, REACH + length :] = right_ref[...].astype(jnp.float32)
    nothing = jnp.zeros((rows + 2, REACH, width), jnp.float32)

    @pl.when(slab == 0)
    def _():
        grid_s[0] = jnp.zeros(grid_s.shape[1:], jnp.float32)

    @pl.when(slab == lax.axis_size("slab") - 1)
    def _():
        grid_s[1 + rows] = jnp.zeros(grid_s.shape[1:], jnp.float32)

    @pl.when(tile == 0)
    def _():
        grid_s[:, :REACH] = nothing

    @pl.when(tile == lax.axis_size("tile") - 1)
    def _():
        grid_s[:, REACH + length :] = nothing

    blocks = length // REACH
    occ_row = slab * rows // BLOCK
    first = tile * (length // BLOCK)
    occ = [occupied_at(occ_ref, occ_row, first - 2 + b) for b in range(2 * blocks + 4)]
    for block in range(blocks):
        bias_s[block] = block_bias(occ[2 * block : 2 * block + 6])
    taps = [[conv_ref[a, pl.ds(b, 1), :] for b in range(3)] for a in range(3)]
    gain = gain_ref[...]
    count = length + 2 * REACH

    def one_row(row, carry):
        above, here, below = grid_s[row], grid_s[row + 1], grid_s[row + 2]
        left, middle, right = (
            taps[0][b] * above + taps[1][b] * here + taps[2][b] * below for b in range(3)
        )
        convolved = here + middle + pltpu.roll(left, 1, 0) + pltpu.roll(right, count - 1, 0)
        stream = convolved.astype(jnp.bfloat16).astype(jnp.float32)
        normed = norm(stream, gain)
        queries, keys, values_t = project(normed, qkv_ref, width)
        for block in range(blocks):
            low = block * REACH
            update = attend_block(
                queries[REACH + low : 2 * REACH + low],
                keys[low : low + KEYS],
                values_t[:, low : low + KEYS],
                bias_s[block],
                occ[2 + 2 * block : 4 + 2 * block],
                out_ref[...],
            )
            result = stream[REACH + low : 2 * REACH + low] + update
            after_s[row, low // cols : (low + REACH) // cols] = result.reshape(
                REACH // cols, cols, width
            ).astype(jnp.bfloat16)
        return carry

    for group in range(rows // GROUP):
        start = group * GROUP
        lax.fori_loop(start, start + GROUP, one_row, 0)
        if group == 0:
            pl.semaphore_wait(barrier, slabs - 1)
        taken = pl.ds(start, GROUP)
        place = pl.ds(slab * rows + start, GROUP)
        pltpu.make_async_copy(
            after_s.at[taken, slab], columns_ref.at[place], own_sem.at[group]
        ).start()

        def send(to):
            pltpu.make_async_remote_copy(
                src_ref=after_s.at[taken, to], dst_ref=columns_ref.at[place],
                send_sem=send_sem, recv_sem=recv_sem, device_id=(to, tile), device_id_type=MESH,
            ).start()

        def send_both(step, carry):
            ahead, behind = slab + step, slab - step
            send(jnp.where(ahead >= slabs, ahead - slabs, ahead))
            send(jnp.where(behind < 0, behind + slabs, behind))
            return carry

        lax.fori_loop(1, slabs // 2, send_both, 0, unroll=3)
        half = slab + slabs // 2
        send(jnp.where(half >= slabs, half - slabs, half))
    for group in range(rows // GROUP):
        start = group * GROUP
        pltpu.make_async_copy(
            after_s.at[pl.ds(start, GROUP), slab],
            columns_ref.at[pl.ds(slab * rows + start, GROUP)],
            own_sem.at[group],
        ).wait()
    sent = columns_ref.at[pl.ds(0, (slabs - 1) * rows)]
    whole = pltpu.make_async_remote_copy(
        src_ref=sent, dst_ref=sent, send_sem=send_sem, recv_sem=recv_sem,
        device_id=(lax.rem(slab + 1, slabs), tile), device_id_type=MESH,
    )
    whole.wait_send()
    whole.wait_recv()


def col_kernel(occ_ref, x_ref, gain_ref, qkv_ref, out_ref, mixed_ref, line_s, query_s, key_s, val_s, blocks_s):
    count, width = x_ref.shape
    cols = key_s.shape[0]
    height = count // cols
    slab, tile = lax.axis_index("slab"), lax.axis_index("tile")
    slabs = lax.axis_size("slab")
    occ_col = (tile * slabs + slab) * cols // BLOCK
    line_s[...] = x_ref[...].astype(jnp.float32)
    gain = gain_ref[...]
    for col in range(cols):
        normed = norm(line_s[pl.ds(col, height, stride=cols), :], gain)
        query_s[col], keys, values_t = project(normed, qkv_ref, width)
        edge = jnp.zeros((REACH, width), jnp.bfloat16)
        key_s[col, :REACH], key_s[col, REACH + height :] = edge, edge
        key_s[col, REACH : REACH + height] = keys
        wide = jnp.concatenate([edge, values_t, edge], axis=1)
        val_s[0, col] = wide
        val_s[1, col, :, : height + REACH] = wide[:, BLOCK : BLOCK + height + REACH]
        val_s[1, col, :, height + REACH :] = edge

    at = lax.broadcasted_iota(jnp.int32, (SPAN, 128), 0)
    offset = lax.broadcasted_iota(jnp.int32, (SPAN, 128), 1) % BLOCK - (at - REACH)
    band = jnp.where(jnp.abs(offset) < REACH, jnp.float32(0.0), jnp.float32(NEG))

    total_blocks = height // BLOCK

    def note(block, found):
        blocks_s[found] = block
        return found + jnp.where(occupied_at(occ_ref, block, occ_col) > 0, 1, 0)

    found = lax.fori_loop(0, total_blocks, note, 0)

    @pl.when(found < total_blocks)
    def _():
        blocks_s[found] = 0

    def updates_of(block):
        occ = [occupied_at(occ_ref, block - 2 + b, occ_col) for b in range(5)]
        barred = [
            jnp.full((BLOCK, 128), jnp.where(value > 0, jnp.float32(0.0), jnp.float32(NEG)))
            for value in occ
        ]
        bias = jnp.where(offset == 0, 0.0, jnp.minimum(band, jnp.concatenate(barred, axis=0)))
        low = pl.multiple_of(block * BLOCK, BLOCK)
        wide_low = pl.multiple_of(block // 2 * REACH, REACH)
        return [
            attend_small(
                query_s[col, pl.ds(low, BLOCK)],
                key_s[col, pl.ds(low, SPAN)],
                val_s[block % 2, col, :, pl.ds(wide_low, KEYS)][:, :SPAN],
                bias,
                out_ref[...],
            )
            for col in range(cols)
        ]

    def add(block, updates):
        for col in range(cols):
            place = pl.ds(block * (BLOCK * cols) + col, BLOCK, stride=cols)
            line_s[place, :] = line_s[place, :] + updates[col]

    def two_blocks(pair, carry):
        one, two = blocks_s[2 * pair], blocks_s[2 * pair + 1]
        first, second = updates_of(one), updates_of(two)
        add(one, first)

        @pl.when(2 * pair + 1 < found)
        def _():
            add(two, second)

        return carry

    lax.fori_loop(0, (found + 1) // 2, two_blocks, 0)
    mixed_ref[...] = line_s[...].astype(jnp.bfloat16)


VMEM = pl.BlockSpec(memory_space=pltpu.VMEM)
SMEM = pl.BlockSpec(memory_space=pltpu.SMEM)


ANY = pl.BlockSpec(memory_space=pl.ANY)
MESH = pl.DeviceIdType.MESH


def halo_kernel(own_ref, top_ref, bottom_ref, left_ref, right_ref, send_sem, recv_sem):
    rows, length, width = own_ref.shape
    slabs, tiles = lax.axis_size("slab"), lax.axis_size("tile")
    slab, tile = lax.axis_index("slab"), lax.axis_index("tile")
    down, up = lax.rem(slab + 1, slabs), lax.rem(slab + slabs - 1, slabs)
    east, west = lax.rem(tile + 1, tiles), lax.rem(tile + tiles - 1, tiles)
    low, high = pl.ds(0, REACH), pl.ds(length - REACH, REACH)
    first, last, inner = pl.ds(0, 1), pl.ds(rows - 1, 1), pl.ds(1, rows)
    after = pl.ds(rows + 1, 1)
    plan = [
        (own_ref.at[:, high], left_ref.at[inner], (slab, east)),
        (own_ref.at[:, low], right_ref.at[inner], (slab, west)),
        (own_ref.at[last, high], left_ref.at[first], (down, east)),
        (own_ref.at[last, low], right_ref.at[first], (down, west)),
        (own_ref.at[first, high], left_ref.at[after], (up, east)),
        (own_ref.at[first, low], right_ref.at[after], (up, west)),
        (own_ref.at[last], top_ref, (down, tile)),
        (own_ref.at[first], bottom_ref, (up, tile)),
    ]
    barrier = pltpu.get_barrier_semaphore()
    for _, _, device in plan:
        pl.semaphore_signal(barrier, inc=1, device_id=device, device_id_type=MESH)
    pl.semaphore_wait(barrier, len(plan))
    copies = [
        pltpu.make_async_remote_copy(
            src_ref=source, dst_ref=target, send_sem=send_sem.at[k], recv_sem=recv_sem.at[k],
            device_id=device, device_id_type=MESH,
        )
        for k, (source, target, device) in enumerate(plan)
    ]
    for copy in copies:
        copy.start()
    for copy in copies:
        copy.wait()


def local(tokens, conv_weight, occupancy, row_gain, row_qkv, row_out, col_gain, col_qkv, col_out):
    rows, length, width = tokens.shape
    slabs = lax.axis_size("slab")
    cols = length // slabs
    height = rows * slabs
    count = length + 2 * REACH
    edge = jax.ShapeDtypeStruct((1, length, width), tokens.dtype)
    side = jax.ShapeDtypeStruct((rows + 2, REACH, width), tokens.dtype)
    top, bottom, left, right = pl.pallas_call(
        halo_kernel,
        out_shape=(edge, edge, side, side),
        in_specs=[ANY],
        out_specs=(ANY,) * 4,
        scratch_shapes=[pltpu.SemaphoreType.DMA((8,)), pltpu.SemaphoreType.DMA((8,))],
        compiler_params=pltpu.CompilerParams(collective_id=0, has_side_effects=True),
        name="halo",
    )(tokens)
    columns = pl.pallas_call(
        row_kernel,
        out_shape=jax.ShapeDtypeStruct((height, cols, width), jnp.bfloat16),
        in_specs=[SMEM] + [VMEM] * 9,
        out_specs=ANY,
        scratch_shapes=[
            pltpu.VMEM((rows + 2, count, width), jnp.float32),
            pltpu.VMEM((length // REACH, KEYS, REACH), jnp.float32),
            pltpu.VMEM((rows, slabs, cols, width), jnp.bfloat16),
            pltpu.SemaphoreType.DMA((rows // GROUP,)),
            pltpu.SemaphoreType.DMA,
            pltpu.SemaphoreType.DMA,
        ],
        compiler_params=pltpu.CompilerParams(collective_id=1, has_side_effects=True),
        name="row_sublayer",
    )(
        occupancy, tokens, top, bottom, left, right,
        conv_weight, row_gain.reshape(1, width), row_qkv, row_out,
    )
    mixed = pl.pallas_call(
        col_kernel,
        out_shape=jax.ShapeDtypeStruct((height * cols, width), jnp.bfloat16),
        in_specs=[SMEM] + [VMEM] * 4,
        out_specs=VMEM,
        scratch_shapes=[
            pltpu.VMEM((height * cols, width), jnp.float32),
            pltpu.VMEM((cols, height, width), jnp.bfloat16),
            pltpu.VMEM((cols, height + 2 * REACH, width), jnp.bfloat16),
            pltpu.VMEM((2, cols, width, height + 2 * REACH), jnp.bfloat16),
            pltpu.SMEM((height // BLOCK,), jnp.int32),
        ],
        name="col_sublayer",
    )(occupancy, columns.reshape(height * cols, width), col_gain.reshape(1, width), col_qkv, col_out)
    return mixed.reshape(height, cols, width)


def solution(mesh):
    return jax.shard_map(
        local,
        mesh=mesh,
        in_specs=(P("slab", "tile", None), P(), P(), P(), P(), P(), P(), P(), P()),
        out_specs=P(None, ("tile", "slab"), None),
        check_vma=False,
    )
```

```python
import math

import jax
import jax.numpy as jnp
from jax import lax
from jax.experimental import pallas as pl
from jax.experimental.pallas import tpu as pltpu
from jax.sharding import PartitionSpec as P

HEAD_DIM = 32
HEADS = 4
BLOCK = 64
REACH = 128
KEYS = 3 * REACH
GROUP = 2
NEG = -1e30
SCALE = math.log2(math.e) / math.sqrt(HEAD_DIM)


def norm(values32, gain):
    center = jnp.mean(values32, axis=-1, keepdims=True)
    centered = values32 - center
    spread = jnp.mean(centered * centered, axis=-1, keepdims=True)
    return (centered * lax.rsqrt(spread + 1e-05) * gain).astype(jnp.bfloat16)


def block_bias(key_occupied):
    at = lax.broadcasted_iota(jnp.int32, (KEYS, REACH), 0)
    key_bias = jnp.zeros((KEYS, REACH), jnp.float32)
    for index, occupied in enumerate(key_occupied):
        value = jnp.where(occupied > 0, jnp.float32(0.0), jnp.float32(NEG))
        key_bias = jnp.where(at // BLOCK == index, value, key_bias)
    offset = lax.broadcasted_iota(jnp.int32, (KEYS, REACH), 1) - (at - REACH)
    bias = jnp.where(jnp.abs(offset) < REACH, key_bias, NEG)
    return jnp.where(offset == 0, 0.0, bias)


def attend_block(queries, keys, values_t, bias, query_occupied, out_weight):
    head = lax.broadcasted_iota(jnp.int32, (REACH, 128), 1) // HEAD_DIM
    zero = jnp.zeros_like(queries)
    stacked = jnp.concatenate([jnp.where(head == h, queries, zero) for h in range(HEADS)], axis=0)
    scores = lax.dot_general(
        keys, stacked, (((1,), (1,)), ((), ())), preferred_element_type=jnp.float32
    )
    lane = lax.broadcasted_iota(jnp.int32, (1, REACH), 1)
    occupied = jnp.where(lane < BLOCK, query_occupied[0], query_occupied[1]).astype(jnp.float32)
    mixtures = []
    for h in range(HEADS):
        part = scores[:, h * REACH : (h + 1) * REACH] + bias
        weights = jnp.exp2(part - jnp.max(part, axis=0, keepdims=True))
        total = jnp.sum(weights, axis=0, keepdims=True)
        mixture = jnp.dot(
            values_t[h * HEAD_DIM : (h + 1) * HEAD_DIM],
            weights.astype(jnp.bfloat16),
            preferred_element_type=jnp.float32,
        )
        mixtures.append(mixture * (occupied / total))
    mixture = jnp.concatenate(mixtures, axis=0).T.astype(jnp.bfloat16)
    return jnp.dot(mixture, out_weight, preferred_element_type=jnp.float32)


SPAN = BLOCK + 2 * REACH


def attend_small(queries, keys, values_t, bias, out_weight):
    head = lax.broadcasted_iota(jnp.int32, (BLOCK, 128), 1) // HEAD_DIM
    zero = jnp.zeros_like(queries)
    stacked = jnp.concatenate([jnp.where(head == h, queries, zero) for h in range(HEADS)], axis=0)
    scores = lax.dot_general(
        keys, stacked, (((1,), (1,)), ((), ())), preferred_element_type=jnp.float32
    )
    mixtures = []
    for pair in range(HEADS // 2):
        part = scores[:, pair * 128 : (pair + 1) * 128] + bias
        weights = jnp.exp2(part - jnp.max(part, axis=0, keepdims=True))
        total = jnp.sum(weights, axis=0, keepdims=True)
        mixture = jnp.dot(
            values_t[pair * BLOCK : (pair + 1) * BLOCK],
            weights.astype(jnp.bfloat16),
            preferred_element_type=jnp.float32,
        )
        mixtures.append(mixture * (1.0 / total))
    both = jnp.concatenate(mixtures, axis=0).T
    mixture = jnp.where(head % 2 == 0, both[:BLOCK], both[BLOCK:]).astype(jnp.bfloat16)
    return jnp.dot(mixture, out_weight, preferred_element_type=jnp.float32)


def project(normed, qkv_ref, width):
    both = jnp.dot(normed, qkv_ref[:, : 2 * width], preferred_element_type=jnp.float32)
    values_t = lax.dot_general(
        qkv_ref[:, 2 * width :], normed, (((0,), (1,)), ((), ())), preferred_element_type=jnp.float32
    )
    queries = (both[:, :width] * SCALE).astype(jnp.bfloat16)
    return queries, both[:, width:].astype(jnp.bfloat16), values_t.astype(jnp.bfloat16)


def occupied_at(occ_ref, row, col):
    high, wide = occ_ref.shape
    inside = (row >= 0) & (row < high) & (col >= 0) & (col < wide)
    value = occ_ref[jnp.clip(row, 0, high - 1), jnp.clip(col, 0, wide - 1)]
    return jnp.where(inside, value, 0)


def row_kernel(
    occ_ref, own_ref, top_ref, bottom_ref, left_ref, right_ref, conv_ref, gain_ref, qkv_ref, out_ref,
    columns_ref, grid_s, bias_s, after_s, own_sem, send_sem, recv_sem,
):
    rows, length, width = own_ref.shape
    slabs, cols = after_s.shape[1:3]
    slab, tile = lax.axis_index("slab"), lax.axis_index("tile")
    barrier = pltpu.get_barrier_semaphore()

    def greet(k, carry):
        to = slab + k
        device = (jnp.where(to >= slabs, to - slabs, to), tile)
        pl.semaphore_signal(barrier, inc=1, device_id=device, device_id_type=MESH)
        return carry

    lax.fori_loop(1, slabs, greet, 0)
    grid_s[0, REACH : REACH + length] = top_ref[0].astype(jnp.float32)
    grid_s[1 : 1 + rows, REACH : REACH + length] = own_ref[...].astype(jnp.float32)
    grid_s[1 + rows, REACH : REACH + length] = bottom_ref[0].astype(jnp.float32)
    grid_s[:, :REACH] = left_ref[...].astype(jnp.float32)
    grid_s[:, REACH + length :] = right_ref[...].astype(jnp.float32)
    nothing = jnp.zeros((rows + 2, REACH, width), jnp.float32)

    @pl.when(slab == 0)
    def _():
        grid_s[0] = jnp.zeros(grid_s.shape[1:], jnp.float32)

    @pl.when(slab == lax.axis_size("slab") - 1)
    def _():
        grid_s[1 + rows] = jnp.zeros(grid_s.shape[1:], jnp.float32)

    @pl.when(tile == 0)
    def _():
        grid_s[:, :REACH] = nothing

    @pl.when(tile == lax.axis_size("tile") - 1)
    def _():
        grid_s[:, REACH + length :] = nothing

    blocks = length // REACH
    occ_row = slab * rows // BLOCK
    first = tile * (length // BLOCK)
    occ = [occupied_at(occ_ref, occ_row, first - 2 + b) for b in range(2 * blocks + 4)]
    for block in range(blocks):
        bias_s[block] = block_bias(occ[2 * block : 2 * block + 6])
    taps = [[conv_ref[a, pl.ds(b, 1), :] for b in range(3)] for a in range(3)]
    gain = gain_ref[...]
    count = length + 2 * REACH

    def one_row(row, carry):
        above, here, below = grid_s[row], grid_s[row + 1], grid_s[row + 2]
        left, middle, right = (
            taps[0][b] * above + taps[1][b] * here + taps[2][b] * below for b in range(3)
        )
        convolved = here + middle + pltpu.roll(left, 1, 0) + pltpu.roll(right, count - 1, 0)
        stream = convolved.astype(jnp.bfloat16).astype(jnp.float32)
        normed = norm(stream, gain)
        queries, keys, values_t = project(normed, qkv_ref, width)
        for block in range(blocks):
            low = block * REACH
            update = attend_block(
                queries[REACH + low : 2 * REACH + low],
                keys[low : low + KEYS],
                values_t[:, low : low + KEYS],
                bias_s[block],
                occ[2 + 2 * block : 4 + 2 * block],
                out_ref[...],
            )
            result = stream[REACH + low : 2 * REACH + low] + update
            after_s[row, low // cols : (low + REACH) // cols] = result.reshape(
                REACH // cols, cols, width
            ).astype(jnp.bfloat16)
        return carry

    for group in range(rows // GROUP):
        start = group * GROUP
        lax.fori_loop(start, start + GROUP, one_row, 0)
        if group == 0:
            pl.semaphore_wait(barrier, slabs - 1)
        taken = pl.ds(start, GROUP)
        place = pl.ds(slab * rows + start, GROUP)
        pltpu.make_async_copy(
            after_s.at[taken, slab], columns_ref.at[place], own_sem.at[group]
        ).start()

        def send(to):
            pltpu.make_async_remote_copy(
                src_ref=after_s.at[taken, to], dst_ref=columns_ref.at[place],
                send_sem=send_sem, recv_sem=recv_sem, device_id=(to, tile), device_id_type=MESH,
            ).start()

        def send_both(step, carry):
            away = slabs // 2 - step
            ahead, behind = slab + away, slab - away
            send(jnp.where(ahead >= slabs, ahead - slabs, ahead))
            send(jnp.where(behind < 0, behind + slabs, behind))
            return carry

        half = slab + slabs // 2
        send(jnp.where(half >= slabs, half - slabs, half))
        lax.fori_loop(1, slabs // 2, send_both, 0, unroll=3)
    for group in range(rows // GROUP):
        start = group * GROUP
        pltpu.make_async_copy(
            after_s.at[pl.ds(start, GROUP), slab],
            columns_ref.at[pl.ds(slab * rows + start, GROUP)],
            own_sem.at[group],
        ).wait()
    sent = columns_ref.at[pl.ds(0, (slabs - 1) * rows)]
    whole = pltpu.make_async_remote_copy(
        src_ref=sent, dst_ref=sent, send_sem=send_sem, recv_sem=recv_sem,
        device_id=(lax.rem(slab + 1, slabs), tile), device_id_type=MESH,
    )
    whole.wait_send()
    whole.wait_recv()


def col_kernel(occ_ref, x_ref, gain_ref, qkv_ref, out_ref, mixed_ref, line_s, query_s, key_s, val_s, blocks_s):
    count, width = x_ref.shape
    cols = key_s.shape[0]
    height = count // cols
    slab, tile = lax.axis_index("slab"), lax.axis_index("tile")
    slabs = lax.axis_size("slab")
    occ_col = (tile * slabs + slab) * cols // BLOCK
    line_s[...] = x_ref[...].astype(jnp.float32)
    gain = gain_ref[...]
    for col in range(cols):
        normed = norm(line_s[pl.ds(col, height, stride=cols), :], gain)
        query_s[col], keys, values_t = project(normed, qkv_ref, width)
        edge = jnp.zeros((REACH, width), jnp.bfloat16)
        key_s[col, :REACH], key_s[col, REACH + height :] = edge, edge
        key_s[col, REACH : REACH + height] = keys
        wide = jnp.concatenate([edge, values_t, edge], axis=1)
        val_s[0, col] = wide
        val_s[1, col, :, : height + REACH] = wide[:, BLOCK : BLOCK + height + REACH]
        val_s[1, col, :, height + REACH :] = edge

    at = lax.broadcasted_iota(jnp.int32, (SPAN, 128), 0)
    offset = lax.broadcasted_iota(jnp.int32, (SPAN, 128), 1) % BLOCK - (at - REACH)
    band = jnp.where(jnp.abs(offset) < REACH, jnp.float32(0.0), jnp.float32(NEG))

    total_blocks = height // BLOCK

    def note(block, found):
        blocks_s[found] = block
        return found + jnp.where(occupied_at(occ_ref, block, occ_col) > 0, 1, 0)

    found = lax.fori_loop(0, total_blocks, note, 0)

    @pl.when(found < total_blocks)
    def _():
        blocks_s[found] = 0

    def updates_of(block):
        occ = [occupied_at(occ_ref, block - 2 + b, occ_col) for b in range(5)]
        barred = [
            jnp.full((BLOCK, 128), jnp.where(value > 0, jnp.float32(0.0), jnp.float32(NEG)))
            for value in occ
        ]
        bias = jnp.where(offset == 0, 0.0, jnp.minimum(band, jnp.concatenate(barred, axis=0)))
        low = pl.multiple_of(block * BLOCK, BLOCK)
        wide_low = pl.multiple_of(block // 2 * REACH, REACH)
        return [
            attend_small(
                query_s[col, pl.ds(low, BLOCK)],
                key_s[col, pl.ds(low, SPAN)],
                val_s[block % 2, col, :, pl.ds(wide_low, KEYS)][:, :SPAN],
                bias,
                out_ref[...],
            )
            for col in range(cols)
        ]

    def add(block, updates):
        for col in range(cols):
            place = pl.ds(block * (BLOCK * cols) + col, BLOCK, stride=cols)
            line_s[place, :] = line_s[place, :] + updates[col]

    def two_blocks(pair, carry):
        one, two = blocks_s[2 * pair], blocks_s[2 * pair + 1]
        first, second = updates_of(one), updates_of(two)
        add(one, first)

        @pl.when(2 * pair + 1 < found)
        def _():
            add(two, second)

        return carry

    lax.fori_loop(0, (found + 1) // 2, two_blocks, 0)
    mixed_ref[...] = line_s[...].astype(jnp.bfloat16)


VMEM = pl.BlockSpec(memory_space=pltpu.VMEM)
SMEM = pl.BlockSpec(memory_space=pltpu.SMEM)


ANY = pl.BlockSpec(memory_space=pl.ANY)
MESH = pl.DeviceIdType.MESH


def halo_kernel(own_ref, top_ref, bottom_ref, left_ref, right_ref, send_sem, recv_sem):
    rows, length, width = own_ref.shape
    slabs, tiles = lax.axis_size("slab"), lax.axis_size("tile")
    slab, tile = lax.axis_index("slab"), lax.axis_index("tile")
    down, up = lax.rem(slab + 1, slabs), lax.rem(slab + slabs - 1, slabs)
    east, west = lax.rem(tile + 1, tiles), lax.rem(tile + tiles - 1, tiles)
    low, high = pl.ds(0, REACH), pl.ds(length - REACH, REACH)
    first, last, inner = pl.ds(0, 1), pl.ds(rows - 1, 1), pl.ds(1, rows)
    after = pl.ds(rows + 1, 1)
    plan = [
        (own_ref.at[:, high], left_ref.at[inner], (slab, east)),
        (own_ref.at[:, low], right_ref.at[inner], (slab, west)),
        (own_ref.at[last, high], left_ref.at[first], (down, east)),
        (own_ref.at[last, low], right_ref.at[first], (down, west)),
        (own_ref.at[first, high], left_ref.at[after], (up, east)),
        (own_ref.at[first, low], right_ref.at[after], (up, west)),
        (own_ref.at[last], top_ref, (down, tile)),
        (own_ref.at[first], bottom_ref, (up, tile)),
    ]
    barrier = pltpu.get_barrier_semaphore()
    for _, _, device in plan:
        pl.semaphore_signal(barrier, inc=1, device_id=device, device_id_type=MESH)
    pl.semaphore_wait(barrier, len(plan))
    copies = [
        pltpu.make_async_remote_copy(
            src_ref=source, dst_ref=target, send_sem=send_sem.at[k], recv_sem=recv_sem.at[k],
            device_id=device, device_id_type=MESH,
        )
        for k, (source, target, device) in enumerate(plan)
    ]
    for copy in copies:
        copy.start()
    for copy in copies:
        copy.wait()


def local(tokens, conv_weight, occupancy, row_gain, row_qkv, row_out, col_gain, col_qkv, col_out):
    rows, length, width = tokens.shape
    slabs = lax.axis_size("slab")
    cols = length // slabs
    height = rows * slabs
    count = length + 2 * REACH
    edge = jax.ShapeDtypeStruct((1, length, width), tokens.dtype)
    side = jax.ShapeDtypeStruct((rows + 2, REACH, width), tokens.dtype)
    top, bottom, left, right = pl.pallas_call(
        halo_kernel,
        out_shape=(edge, edge, side, side),
        in_specs=[ANY],
        out_specs=(ANY,) * 4,
        scratch_shapes=[pltpu.SemaphoreType.DMA((8,)), pltpu.SemaphoreType.DMA((8,))],
        compiler_params=pltpu.CompilerParams(collective_id=0, has_side_effects=True),
        name="halo",
    )(tokens)
    columns = pl.pallas_call(
        row_kernel,
        out_shape=jax.ShapeDtypeStruct((height, cols, width), jnp.bfloat16),
        in_specs=[SMEM] + [VMEM] * 9,
        out_specs=ANY,
        scratch_shapes=[
            pltpu.VMEM((rows + 2, count, width), jnp.float32),
            pltpu.VMEM((length // REACH, KEYS, REACH), jnp.float32),
            pltpu.VMEM((rows, slabs, cols, width), jnp.bfloat16),
            pltpu.SemaphoreType.DMA((rows // GROUP,)),
            pltpu.SemaphoreType.DMA,
            pltpu.SemaphoreType.DMA,
        ],
        compiler_params=pltpu.CompilerParams(collective_id=1, has_side_effects=True),
        name="row_sublayer",
    )(
        occupancy, tokens, top, bottom, left, right,
        conv_weight, row_gain.reshape(1, width), row_qkv, row_out,
    )
    mixed = pl.pallas_call(
        col_kernel,
        out_shape=jax.ShapeDtypeStruct((height * cols, width), jnp.bfloat16),
        in_specs=[SMEM] + [VMEM] * 4,
        out_specs=VMEM,
        scratch_shapes=[
            pltpu.VMEM((height * cols, width), jnp.float32),
            pltpu.VMEM((cols, height, width), jnp.bfloat16),
            pltpu.VMEM((cols, height + 2 * REACH, width), jnp.bfloat16),
            pltpu.VMEM((2, cols, width, height + 2 * REACH), jnp.bfloat16),
            pltpu.SMEM((height // BLOCK,), jnp.int32),
        ],
        name="col_sublayer",
    )(occupancy, columns.reshape(height * cols, width), col_gain.reshape(1, width), col_qkv, col_out)
    return mixed.reshape(height, cols, width)


def solution(mesh):
    return jax.shard_map(
        local,
        mesh=mesh,
        in_specs=(P("slab", "tile", None), P(), P(), P(), P(), P(), P(), P(), P()),
        out_specs=P(None, ("tile", "slab"), None),
        check_vma=False,
    )
```
